32 devices in a mesh: seq: 16 (over z, y, x), head: 2 (over core).
Axes of the slice: x: 2, y: 2, z: 4, core: 2. Of those that a mesh axis runs over, the one named last changes fastest.
Arguments:
- tokens: bfloat16 [8192, 1536], P('seq', 'head'), may hold values from -6 to 6
- cotangent: bfloat16 [8192, 1536], P('seq', 'head'), may hold values from -6 to 6
- seg_ids: int32 [8192], P('seq'), may hold values from 0 to 8191, as said below
- carry_flags: int32 [32], P('seq'), may hold values from 0 to 1, as said below
- inner_weight: float32 [1536, 2, 3072], P('seq', None, 'head'), may hold values from -0.15625 to 0.15625
- inner_velocity: float32 [1536, 2, 3072], P('seq', None, 'head'), may hold values from -192 to 192
- inner_average: float32 [1536, 2, 3072], P('seq', None, 'head'), may hold values from -0.15625 to 0.15625
- groups_weight: float32 [1536, 256], P('seq', 'head'), may hold values from -0.15625 to 0.15625
- groups_velocity: float32 [1536, 256], P('seq', 'head'), may hold values from -192 to 192
- groups_average: float32 [1536, 256], P('seq', 'head'), may hold values from -0.15625 to 0.15625
- stepper_weight: float32 [1536, 48], P('seq', 'head'), may hold values from -0.078125 to 0.078125
- stepper_velocity: float32 [1536, 48], P('seq', 'head'), may hold values from -192 to 192
- stepper_average: float32 [1536, 48], P('seq', 'head'), may hold values from -0.078125 to 0.078125
- outer_weight: float32 [3072, 1536], P('head', 'seq'), may hold values from -0.109375 to 0.109375
- outer_velocity: float32 [3072, 1536], P('head', 'seq'), may hold values from -192 to 192
- outer_average: float32 [3072, 1536], P('head', 'seq'), may hold values from -0.109375 to 0.109375
- filters_weight: float32 [5, 3072], P(None, 'head'), may hold values from -3 to 3
- filters_velocity: float32 [5, 3072], P(None, 'head'), may hold values from -192 to 192
- filters_average: float32 [5, 3072], P(None, 'head'), may hold values from -3 to 3
- probes_weight: float32 [5, 256], P(None, 'head'), may hold values from -3 to 3
- probes_velocity: float32 [5, 256], P(None, 'head'), may hold values from -192 to 192
- probes_average: float32 [5, 256], P(None, 'head'), may hold values from -3 to 3
- prenorm_weight: float32 [1536], replicated, may hold values from 0.5 to 1.5
- prenorm_velocity: float32 [1536], replicated, may hold values from -192 to 192
- prenorm_average: float32 [1536], replicated, may hold values from -1 to 1
- postnorm_weight: float32 [3072], P('head'), may hold values from 0.5 to 1.5
- postnorm_velocity: float32 [3072], P('head'), may hold values from -192 to 192
- postnorm_average: float32 [3072], P('head'), may hold values from -1 to 1
- heads_weight: float32 [3, 48], P(None, 'head')
- heads_velocity: float32 [3, 48], P(None, 'head'), may hold values from -192 to 192
- heads_average: float32 [3, 48], P(None, 'head'), may hold values from -1 to 1
Outputs:
- output: bfloat16 [8192, 1536], P('seq', 'head')
- input_gradient: float32 [8192, 1536], P('seq', 'head')
- inner_gradient: float32 [1536, 2, 3072], P('seq', None, 'head')
- inner_master: float32 [1536, 2, 3072], P('seq', None, 'head')
- inner_momentum: float32 [1536, 2, 3072], P('seq', None, 'head')
- inner_smoothed: float32 [1536, 2, 3072], P('seq', None, 'head')
- groups_gradient: float32 [1536, 256], P('seq', 'head')
- groups_master: float32 [1536, 256], P('seq', 'head')
- groups_momentum: float32 [1536, 256], P('seq', 'head')
- groups_smoothed: float32 [1536, 256], P('seq', 'head')
- stepper_gradient: float32 [1536, 48], P('seq', 'head')
- stepper_master: float32 [1536, 48], P('seq', 'head')
- stepper_momentum: float32 [1536, 48], P('seq', 'head')
- stepper_smoothed: float32 [1536, 48], P('seq', 'head')
- outer_gradient: float32 [3072, 1536], P('head', 'seq')
- outer_master: float32 [3072, 1536], P('head', 'seq')
- outer_momentum: float32 [3072, 1536], P('head', 'seq')
- outer_smoothed: float32 [3072, 1536], P('head', 'seq')
- filters_gradient: float32 [5, 3072], P(None, 'head')
- filters_master: float32 [5, 3072], P(None, 'head')
- filters_momentum: float32 [5, 3072], P(None, 'head')
- filters_smoothed: float32 [5, 3072], P(None, 'head')
- probes_gradient: float32 [5, 256], P(None, 'head')
- probes_master: float32 [5, 256], P(None, 'head')
- probes_momentum: float32 [5, 256], P(None, 'head')
- probes_smoothed: float32 [5, 256], P(None, 'head')
- prenorm_gradient: float32 [1536], replicated
- prenorm_master: float32 [1536], replicated
- prenorm_momentum: float32 [1536], replicated
- prenorm_smoothed: float32 [1536], replicated
- postnorm_gradient: float32 [3072], P('head')
- postnorm_master: float32 [3072], P('head')
- postnorm_momentum: float32 [3072], P('head')
- postnorm_smoothed: float32 [3072], P('head')
- heads_gradient: float32 [3, 48], P(None, 'head')
- heads_master: float32 [3, 48], P(None, 'head')
- heads_momentum: float32 [3, 48], P(None, 'head')
- heads_smoothed: float32 [3, 48], P(None, 'head')
The draws below stay inside these ranges and needn't reach their ends.
Inputs may be any that keep to these rules, and one draw needn't show every extreme that they name: seg_ids[t] is the position of the first token of t's document, so it never falls; a new document begins at every multiple of 8192 and at the last token. carry_flags[c] is 0 where a document begins at token c * 256, else 1.
All inputs are finite; a program needn't handle non-finite values.
Results may differ from the reference program's by a relative error of at most 0.0038.
The reference program's roundings to bfloat16 on the way count: a program that leaves them out, or rounds other values in their place, can miss the bound.
Values may be sent and summed in bfloat16 or wider, within the bound.
No kernel may reach another device: no remote copies, remote signals or barrier semaphores. Data moves between devices by JAX's collectives and lax.ppermute only.
A program may use at most 256 MiB of HBM per device.

```python
import math
import jax
import jax.numpy as jnp
from jax import lax

D = 1536
DI = 3072
H = 48
P_SIZE = 64
N = 128
KC = 4
CH = 256
TOK_DEV = 512
SEQS = 1
TOKENS = 8192
LENGTH = 8192


def document_starts(key):
    base = jax.random.fold_in(key, 17)
    first_key, second_key, third_key = jax.random.split(base, 3)
    regions = 64
    exponents = jax.random.randint(first_key, (regions,), 3, 16)
    per_token = jnp.repeat(exponents, TOKENS // regions)
    drawn = jax.random.randint(second_key, (TOKENS,), 0, 32768)
    starts = drawn % jnp.left_shift(jnp.ones_like(per_token), per_token) == 0
    coins = jnp.repeat(jax.random.randint(third_key, (TOKENS // CH,), 0, 4) == 0, CH)
    positions = jnp.arange(TOKENS)
    starts = starts | coins & (positions % CH == 0)
    entries = jnp.abs(positions - TOKENS // 2) < 2 * TOK_DEV
    starts = starts & jnp.logical_not(entries)
    starts = starts | (positions % LENGTH == 0) | (positions == TOKENS - 1)
    return starts.astype(jnp.int32)


def draw_seg_ids(key, part):
    positions = jnp.arange(TOKENS).astype(jnp.int32)
    marked = jnp.where(document_starts(key) == 1, positions, jnp.zeros_like(positions))
    return lax.cummax(marked, axis=0).astype(jnp.int32)


def draw_carry_flags(key, part):
    return (1 - document_starts(key)[::CH]).astype(jnp.int32)


def draw_heads_weight(key, part):
    base = jax.random.fold_in(key, 23)
    first_key, second_key, third_key = jax.random.split(base, 3)
    step_sizes = jnp.exp(jax.random.uniform(first_key, (H,), jnp.float32, math.log(0.003), math.log(0.1)))
    log_rates = jax.random.uniform(second_key, (H,), jnp.float32, -9.0, 3.0)
    skip_gains = jax.random.uniform(third_key, (H,), jnp.float32, 0.5, 1.5)
    step_bias = step_sizes + jnp.log(-jnp.expm1(-step_sizes))
    return jnp.stack([step_bias, log_rates, skip_gains]).astype(jnp.float32)


def block_scale(key, extent, cuts, low, top_value):
    level = 1.0
    for dim, parts in cuts:
        draws = jax.random.uniform(jax.random.fold_in(jax.random.fold_in(key, 6), dim), (parts,), jnp.float32, low / len(cuts), top_value / len(cuts))
        level = level * jnp.repeat(jnp.exp(draws), extent[dim] // parts).reshape((-1,) + (1,) * (len(extent) - 1 - dim))
    return level


def gaussian(own_key, shape, deviation, reach, cuts=(), dtype=jnp.bfloat16):
    values = jax.random.normal(own_key, shape, jnp.float32) * deviation
    if len(cuts) > 0:
        values = block_scale(own_key, shape, cuts, -0.22, 0.18) * values
    return jnp.clip(values, min=-reach, max=reach).astype(dtype)


def setup_inputs(seed: int = 0) -> dict:
    arg_keys = jax.random.split(jax.random.key(seed), 32)
    tokens = gaussian(arg_keys[0], (TOKENS, D), 1.0, 6.0, ((0, 16), (1, 2)))
    cotangent = gaussian(arg_keys[1], (TOKENS, D), 1.0, 6.0, ((0, 16), (1, 2)))
    seg_ids = draw_seg_ids(jax.random.fold_in(arg_keys[31], 71), 0)
    carry_flags = draw_carry_flags(jax.random.fold_in(arg_keys[31], 71), 0)
    inner_weight = gaussian(arg_keys[4], (D, 2, DI), D ** -0.5, 0.15625, ((0, 16), (2, 2)), jnp.float32)
    inner_velocity = gaussian(arg_keys[5], (D, 2, DI), (TOKENS ** 0.5 / 3), 192.0, ((0, 16), (2, 2)), jnp.float32)
    inner_average = gaussian(arg_keys[6], (D, 2, DI), D ** -0.5, 0.15625, ((0, 16), (2, 2)), jnp.float32)
    groups_weight = gaussian(arg_keys[7], (D, 2 * N), D ** -0.5, 0.15625, ((0, 16), (1, 2)), jnp.float32)
    groups_velocity = gaussian(arg_keys[8], (D, 2 * N), (TOKENS ** 0.5 / 3), 192.0, ((0, 16), (1, 2)), jnp.float32)
    groups_average = gaussian(arg_keys[9], (D, 2 * N), D ** -0.5, 0.15625, ((0, 16), (1, 2)), jnp.float32)
    stepper_weight = gaussian(arg_keys[10], (D, H), (4 * D) ** -0.5, 0.078125, ((0, 16), (1, 2)), jnp.float32)
    stepper_velocity = gaussian(arg_keys[11], (D, H), (TOKENS ** 0.5 / 3), 192.0, ((0, 16), (1, 2)), jnp.float32)
    stepper_average = gaussian(arg_keys[12], (D, H), (4 * D) ** -0.5, 0.078125, ((0, 16), (1, 2)), jnp.float32)
    outer_weight = gaussian(arg_keys[13], (DI, D), DI ** -0.5, 0.109375, ((0, 2), (1, 16)), jnp.float32)
    outer_velocity = gaussian(arg_keys[14], (DI, D), (TOKENS ** 0.5 / 3), 192.0, ((0, 2), (1, 16)), jnp.float32)
    outer_average = gaussian(arg_keys[15], (DI, D), DI ** -0.5, 0.109375, ((0, 2), (1, 16)), jnp.float32)
    filters_weight = gaussian(arg_keys[16], (KC + 1, DI), KC ** -0.5, 3.0, ((1, 2),), jnp.float32)
    filters_velocity = gaussian(arg_keys[17], (KC + 1, DI), (TOKENS ** 0.5 / 3), 192.0, ((1, 2),), jnp.float32)
    filters_average = gaussian(arg_keys[18], (KC + 1, DI), KC ** -0.5, 3.0, ((1, 2),), jnp.float32)
    probes_weight = gaussian(arg_keys[19], (KC + 1, 2 * N), KC ** -0.5, 3.0, ((1, 2),), jnp.float32)
    probes_velocity = gaussian(arg_keys[20], (KC + 1, 2 * N), (TOKENS ** 0.5 / 3), 192.0, ((1, 2),), jnp.float32)
    probes_average = gaussian(arg_keys[21], (KC + 1, 2 * N), KC ** -0.5, 3.0, ((1, 2),), jnp.float32)
    prenorm_weight = jnp.clip(1.0 + 0.1 * jax.random.normal(arg_keys[22], (D,), jnp.float32), 0.5, 1.5)
    prenorm_velocity = gaussian(arg_keys[23], (D,), (TOKENS ** 0.5 / 3), 192.0, (), jnp.float32)
    prenorm_average = jnp.clip(jax.random.uniform(arg_keys[24], (D,), jnp.float32, -1.0, 1.0), -1.0, 1.0)
    postnorm_weight = jnp.clip(1.0 + 0.1 * jax.random.normal(arg_keys[25], (DI,), jnp.float32), 0.5, 1.5)
    postnorm_velocity = gaussian(arg_keys[26], (DI,), (TOKENS ** 0.5 / 3), 192.0, ((0, 2),), jnp.float32)
    postnorm_average = jnp.clip(jax.random.uniform(arg_keys[27], (DI,), jnp.float32, -1.0, 1.0) * block_scale(arg_keys[27], (DI,), ((0, 2),), -0.4, 0.0), -1.0, 1.0)
    heads_weight = draw_heads_weight(jax.random.fold_in(arg_keys[31], 71), 0)
    heads_velocity = gaussian(arg_keys[29], (3, H), (TOKENS ** 0.5 / 3), 192.0, ((1, 2),), jnp.float32)
    heads_average = jnp.clip(jax.random.uniform(arg_keys[30], (3, H), jnp.float32, -1.0, 1.0) * block_scale(arg_keys[30], (3, H), ((1, 2),), -0.4, 0.0), -1.0, 1.0)
    return {"tokens": tokens, "cotangent": cotangent, "seg_ids": seg_ids, "carry_flags": carry_flags, "inner_weight": inner_weight, "inner_velocity": inner_velocity, "inner_average": inner_average, "groups_weight": groups_weight, "groups_velocity": groups_velocity, "groups_average": groups_average, "stepper_weight": stepper_weight, "stepper_velocity": stepper_velocity, "stepper_average": stepper_average, "outer_weight": outer_weight, "outer_velocity": outer_velocity, "outer_average": outer_average, "filters_weight": filters_weight, "filters_velocity": filters_velocity, "filters_average": filters_average, "probes_weight": probes_weight, "probes_velocity": probes_velocity, "probes_average": probes_average, "prenorm_weight": prenorm_weight, "prenorm_velocity": prenorm_velocity, "prenorm_average": prenorm_average, "postnorm_weight": postnorm_weight, "postnorm_velocity": postnorm_velocity, "postnorm_average": postnorm_average, "heads_weight": heads_weight, "heads_velocity": heads_velocity, "heads_average": heads_average}


epsilon = 1e-05
momentum_decay = 0.9
average_decay = 0.9
highest = lax.Precision.HIGHEST

@jax.custom_vjp
def low(v):
    return lax.optimization_barrier(v.astype(jnp.bfloat16)).astype(jnp.float32)

@jax.custom_vjp
def low_back(v):
    return v

def low_keep(v):
    return (low(v), None)

def low_pass(kept, grad):
    return (grad,)

def back_keep(v):
    return (v, None)

def back_low(kept, grad):
    return (low(grad),)
low.defvjp(low_keep, low_pass)
low_back.defvjp(back_keep, back_low)

def tap_masks(seg_rows, flag_rows, span_len, taps):
    number = seg_rows.shape[0]
    within = jnp.arange(number) % span_len
    first_seg = jnp.repeat(seg_rows[::span_len], span_len)
    continued = (jnp.repeat(flag_rows, span_len) == 1) & (seg_rows == first_seg)
    stacked = []
    for lagged in range(1, taps):
        earlier = jnp.concatenate([jnp.full((lagged,), -1, jnp.int32), seg_rows[:-lagged]])
        stacked.append(jnp.where(within >= lagged, earlier == seg_rows, continued))
    return jnp.stack(stacked).astype(jnp.float32)

def conv_apply(extended, tap_rows, masks, taps):
    number = extended.shape[0] - (taps - 1)
    total = tap_rows[taps] + tap_rows[0] * extended[taps - 1:]
    for lagged in range(1, taps):
        begin = taps - 1 - lagged
        total = total + tap_rows[lagged] * masks[lagged - 1][:, None] * extended[begin:begin + number]
    return total

def span_step(span_state, pieces, skip_gain):
    values, b_rows, c_rows, step_size, log_decay, seg_rows, flag_value = pieces
    length = seg_rows.shape[0]
    cumulative = jnp.cumsum(log_decay, 0)
    causal = jnp.arange(length)[:, None] >= jnp.arange(length)[None, :]
    within = (causal & (seg_rows[:, None] == seg_rows[None, :]))[:, :, None]
    spread = cumulative[:, None, :] - cumulative[None, :, :]
    decays = jnp.where(within, jnp.exp(jnp.where(within, spread, 0.0)), 0.0)
    scores = jnp.dot(c_rows, b_rows.T, precision=highest)
    mixing = low(scores[:, :, None] * decays * step_size[None, :, :])
    local_part = jnp.einsum('ijh,jhp->ihp', mixing, values, precision=highest)
    carried = flag_value.astype(jnp.float32) * (seg_rows == seg_rows[0]).astype(jnp.float32)
    keeping = (seg_rows == seg_rows[-1]).astype(jnp.float32)
    entering = carried[:, None] * jnp.exp(cumulative)
    carried_part = entering[:, :, None] * jnp.einsum('in,hnp->ihp', c_rows, span_state, precision=highest)
    outputs = local_part + carried_part + skip_gain[None, :, None] * values
    leaving = keeping[:, None] * jnp.exp(cumulative[-1][None, :] - cumulative) * step_size
    chained = carried[-1] * jnp.exp(cumulative[-1])
    new_state = chained[:, None, None] * span_state + jnp.einsum('jn,jhp->hnp', b_rows, values * leaving[:, :, None], precision=highest)
    return (new_state, outputs)

def layer_forward(token_rows, inner, groups, stepper, outer, filters, probes, prenorm, postnorm, heads, seg_ids, carry_flags):
    inner_low = low(inner)
    groups_low = low(groups)
    stepper_low = low(stepper)
    outer_low = low(outer)
    tap_rows = jnp.concatenate([filters, probes], 1)
    skip_gain = heads[2]
    decay_rate = -jnp.exp(heads[1])
    span_total = LENGTH // CH

    def span_fn(span_state, pieces):
        return span_step(span_state, pieces, skip_gain)

    def one_sequence(unused, pieces):
        rows, seg_seq, flag_seq = pieces
        inverse = lax.rsqrt(lax.optimization_barrier(jnp.mean(rows * rows, -1, keepdims=True)) + epsilon)
        normed = low(rows * inverse * prenorm)
        both = jnp.einsum('td,dkc->tkc', normed, inner_low, precision=highest)
        gate_pre = low_back(both[:, 0])
        value_in = low(low_back(both[:, 1]))
        group_in = low(low_back(jnp.dot(normed, groups_low, precision=highest)))
        step_raw = low_back(jnp.dot(normed, stepper_low, precision=highest))
        conv_in = jnp.concatenate([value_in, group_in], 1)
        masks = tap_masks(seg_seq, flag_seq, CH, KC)
        extended = jnp.concatenate([jnp.zeros((KC - 1, conv_in.shape[1]), jnp.float32), conv_in], 0)
        activated = jax.nn.silu(conv_apply(extended, tap_rows, masks, KC))
        values = low(activated[:, :DI]).reshape(span_total, CH, H, P_SIZE)
        b_rows = low(activated[:, DI:DI + N]).reshape(span_total, CH, N)
        c_rows = low(activated[:, DI + N:]).reshape(span_total, CH, N)
        step_size = jax.nn.softplus(step_raw + heads[0])
        log_decay = step_size * decay_rate
        spans = (values, b_rows, c_rows, step_size.reshape(span_total, CH, H), log_decay.reshape(span_total, CH, H), seg_seq.reshape(span_total, CH), flag_seq)
        final_state, ssd_spans = lax.scan(jax.checkpoint(span_fn), jnp.zeros((H, N, P_SIZE), jnp.float32), spans)
        ssd_out = low_back(ssd_spans.reshape(LENGTH, DI))
        gated = ssd_out * jax.nn.silu(gate_pre)
        scale = lax.rsqrt(lax.optimization_barrier(jnp.mean(gated * gated, -1, keepdims=True)) + epsilon)
        mixed = low(gated * scale * postnorm)
        return (unused, rows + jnp.dot(mixed, outer_low, precision=highest))
    stacked = (token_rows.reshape(SEQS, LENGTH, D), seg_ids.reshape(SEQS, LENGTH), carry_flags.reshape(SEQS, LENGTH // CH))
    unused, outputs = lax.scan(jax.checkpoint(one_sequence), jnp.zeros((), jnp.float32), stacked)
    return outputs.reshape(TOKENS, D)

def reference(tokens, cotangent, seg_ids, carry_flags, inner_weight, inner_velocity, inner_average, groups_weight, groups_velocity, groups_average, stepper_weight, stepper_velocity, stepper_average, outer_weight, outer_velocity, outer_average, filters_weight, filters_velocity, filters_average, probes_weight, probes_velocity, probes_average, prenorm_weight, prenorm_velocity, prenorm_average, postnorm_weight, postnorm_velocity, postnorm_average, heads_weight, heads_velocity, heads_average):

    def wrapped(token_rows, inner, groups, stepper, outer, filters, probes, prenorm, postnorm, heads):
        return layer_forward(token_rows, inner, groups, stepper, outer, filters, probes, prenorm, postnorm, heads, seg_ids, carry_flags)
    result, pullback = jax.vjp(wrapped, tokens.astype(jnp.float32), inner_weight, groups_weight, stepper_weight, outer_weight, filters_weight, probes_weight, prenorm_weight, postnorm_weight, heads_weight)
    gradients = pullback(cotangent.astype(jnp.float32))
    root = math.sqrt(TOKENS)
    spreads = [D ** (-0.5), D ** (-0.5), (4 * D) ** (-0.5), DI ** (-0.5), 0.5, 0.5, 0.1, 0.1, 0.5]
    masters = [inner_weight, groups_weight, stepper_weight, outer_weight, filters_weight, probes_weight, prenorm_weight, postnorm_weight, heads_weight]
    velocities = [inner_velocity, groups_velocity, stepper_velocity, outer_velocity, filters_velocity, probes_velocity, prenorm_velocity, postnorm_velocity, heads_velocity]
    averages = [inner_average, groups_average, stepper_average, outer_average, filters_average, probes_average, prenorm_average, postnorm_average, heads_average]
    updates = []
    for position in range(9):
        gradient = gradients[position + 1]
        moment = momentum_decay * velocities[position] + gradient
        stepped = masters[position] - spreads[position] / root * (gradient + momentum_decay * moment)
        smoothed = average_decay * averages[position] + (1.0 - average_decay) * stepped
        updates.append((gradient, stepped, moment, smoothed))
    return (result.astype(jnp.bfloat16), gradients[0], updates[0][0], updates[0][1], updates[0][2], updates[0][3], updates[1][0], updates[1][1], updates[1][2], updates[1][3], updates[2][0], updates[2][1], updates[2][2], updates[2][3], updates[3][0], updates[3][1], updates[3][2], updates[3][3], updates[4][0], updates[4][1], updates[4][2], updates[4][3], updates[5][0], updates[5][1], updates[5][2], updates[5][3], updates[6][0], updates[6][1], updates[6][2], updates[6][3], updates[7][0], updates[7][1], updates[7][2], updates[7][3], updates[8][0], updates[8][1], updates[8][2], updates[8][3])
```

```python
import math

import jax
import jax.numpy as jnp
from jax import lax
from jax.experimental import pallas as pl
from jax.experimental.pallas import tpu as pltpu
from jax.sharding import PartitionSpec as P

D = 1536
DI = 3072
P_SIZE = 64
N = 128
KC = 4
CH = 256
HB = 8


epsilon = 1e-05
momentum_decay = 0.9
average_decay = 0.9
highest = lax.Precision.HIGHEST
f32 = jnp.float32
bf16 = jnp.bfloat16


def shifted(array, axis, by):
    count = lax.axis_size(axis)
    pairs = [(i, i + by) for i in range(count) if 0 <= i + by < count]
    return lax.ppermute(array, axis, pairs)


def swap(array, axis, mask):
    count = lax.axis_size(axis)
    return lax.ppermute(array, axis, [(i, i ^ mask) for i in range(count)])


def bit_orders(axis):
    bits = lax.axis_size(axis).bit_length() - 1
    first = list(range(bits))
    second = first[:]
    if bits > 1:
        second[0], second[1] = 1, 0
    return first, second


def gather_rows(rows, axis, order):
    place = lax.axis_index(axis)
    done = []
    held = rows
    for bit in reversed(order):
        other = swap(held, axis, 1 << bit)
        upper = ((place >> bit) & 1) == 1
        where = sum(1 for b in done if b > bit)
        held = jnp.stack(
            [jnp.where(upper, other, held), jnp.where(upper, held, other)], where
        )
        done.append(bit)
    return held.reshape((lax.axis_size(axis) * rows.shape[0],) + rows.shape[1:])


def scatter_rows(rows, axis, order):
    place = lax.axis_index(axis)
    count = lax.axis_size(axis)
    left = sorted(order, reverse=True)
    held = rows.reshape((2,) * len(left) + (rows.shape[0] // count,) + rows.shape[1:])
    for bit in order:
        where = left.index(bit)
        mine = (place >> bit) & 1
        sent = lax.dynamic_index_in_dim(held, 1 - mine, where, False).astype(bf16)
        kept = lax.dynamic_index_in_dim(held, mine, where, False)
        held = kept.astype(f32) + swap(sent, axis, 1 << bit).astype(f32)
        left.remove(bit)
    return held


def gather_two(rows, axis):
    half = rows.shape[1] // 2
    first, second = bit_orders(axis)
    return gather_rows(rows[:, :half], axis, first), gather_rows(rows[:, half:], axis, second)


def scatter_two(one, two, axis):
    first, second = bit_orders(axis)
    return jnp.concatenate(
        [scatter_rows(one, axis, first), scatter_rows(two, axis, second)], 1
    )


def butterfly_sum(array, axis):
    for bit in range(lax.axis_size(axis).bit_length() - 1):
        array = array + swap(array, axis, 1 << bit)
    return array


def side_by_side(own, other, upper):
    return jnp.concatenate([jnp.where(upper, other, own), jnp.where(upper, own, other)], 1)


def expand(array):
    count = array.shape[-1]
    spread = (
        jnp.arange(count)[:, None] == (jnp.arange(count * P_SIZE) // P_SIZE)[None, :]
    ).astype(f32)
    return jnp.dot(array, spread, precision=highest)


def head_sums(array):
    width = array.shape[-1]
    pick = (
        (jnp.arange(width) // P_SIZE)[:, None] == jnp.arange(width // P_SIZE)[None, :]
    ).astype(f32)
    return jnp.dot(array, pick, precision=highest)


def silu_slope(values):
    sigmoid = jax.nn.sigmoid(values)
    return sigmoid * (1.0 + values * (1.0 - sigmoid))


def tap_masks(seg_rows, flag_rows, span_len, taps):
    number = seg_rows.shape[0]
    within = jnp.arange(number) % span_len
    first_seg = jnp.repeat(seg_rows[::span_len], span_len)
    continued = (jnp.repeat(flag_rows, span_len) == 1) & (seg_rows == first_seg)
    stacked = []
    for lagged in range(1, taps):
        earlier = jnp.concatenate([jnp.full((lagged,), -1, jnp.int32), seg_rows[:-lagged]])
        stacked.append(jnp.where(within >= lagged, earlier == seg_rows, continued))
    return jnp.stack(stacked).astype(jnp.float32)


def conv_apply(extended, tap_rows, masks, taps):
    number = extended.shape[0] - (taps - 1)
    total = tap_rows[taps] + tap_rows[0] * extended[taps - 1 :]
    for lagged in range(1, taps):
        begin = taps - 1 - lagged
        total = (
            total + tap_rows[lagged] * masks[lagged - 1][:, None] * extended[begin : begin + number]
        )
    return total


def conv_backward(extended, tap_rows, masks, grads, taps):
    number = grads.shape[0]
    tap_grads = [jnp.sum(grads * extended[taps - 1 :], 0)]
    ext_grad = jnp.pad(tap_rows[0] * grads, ((taps - 1, 0), (0, 0)))
    for lagged in range(1, taps):
        masked = masks[lagged - 1][:, None] * grads
        begin = taps - 1 - lagged
        tap_grads.append(jnp.sum(masked * extended[begin : begin + number], 0))
        ext_grad = ext_grad + jnp.pad(tap_rows[lagged] * masked, ((begin, lagged), (0, 0)))
    tap_grads.append(jnp.sum(grads, 0))
    return (jnp.stack(tap_grads), ext_grad)


def span_edges(log_decay, seg_spans, flag_spans):
    length = log_decay.shape[1]
    lower = (jnp.arange(length)[:, None] >= jnp.arange(length)[None, :]).astype(f32)
    cumulative = jnp.einsum("ij,cjh->cih", lower, log_decay, precision=highest)
    carried = flag_spans.astype(jnp.float32)[:, None] * (seg_spans == seg_spans[:, :1]).astype(
        jnp.float32
    )
    keeping = (seg_spans == seg_spans[:, -1:]).astype(jnp.float32)
    entering = carried[:, :, None] * jnp.exp(cumulative)
    leaving = keeping[:, :, None] * jnp.exp(cumulative[:, -1:, :] - cumulative)
    chained = carried[:, -1:] * jnp.exp(cumulative[:, -1, :])
    return (cumulative, entering, leaving, chained)


def apply_update(master, velocity, average, gradient, rate_value):
    moment = momentum_decay * velocity + gradient
    stepped = master - rate_value * (gradient + momentum_decay * moment)
    smoothed = average_decay * average + (1.0 - average_decay) * stepped
    return (gradient, stepped, moment, smoothed)


def walk_kernel(count, reverse, part_ref, factor_ref, out_ref):
    def one(turn, state):
        source = count - 1 - turn if reverse else turn
        out_ref[source] = state
        return factor_ref[source] * state + part_ref[source]

    lax.fori_loop(0, count, one, jnp.zeros(part_ref.shape[1:], f32))


def carried_in(part, factors, axis, reverse):
    count = lax.axis_size(axis)
    pieces = part.reshape((count, part.shape[0] // count) + part.shape[1:])
    pieces = lax.all_to_all(pieces, axis, 0, 0)
    walked = pl.pallas_call(
        lambda *refs: walk_kernel(count, reverse, *refs),
        out_shape=jax.ShapeDtypeStruct(pieces.shape, f32),
        name="walk",
    )(pieces, factors)
    return lax.all_to_all(walked, axis, 0, 0).reshape(part.shape)


def masked_bias(seg_row, seg_col):
    length = seg_row.shape[1]
    rows = lax.broadcasted_iota(jnp.int32, (length, length), 0)
    cols = lax.broadcasted_iota(jnp.int32, (length, length), 1)
    return jnp.where((rows >= cols) & (seg_col == seg_row), 0.0, -1e30).astype(f32)


def inner_product(one, two):
    return lax.dot_general(one, two, (((1,), (1,)), ((), ())), preferred_element_type=f32)


def span_kernel(cum_ref, step_ref, seg_row_ref, seg_col_ref, b_ref, c_ref, v_ref, skip_ref, y_ref,
                scores_ref, bias_ref):
    @pl.when(pl.program_id(1) == 0)
    def _():
        scores_ref[...] = inner_product(c_ref[...], b_ref[...])
        bias_ref[...] = masked_bias(seg_row_ref[...], seg_col_ref[...])

    cum_rows = cum_ref[...]
    cum_cols = cum_rows.T
    step_rows = step_ref[...]
    low_lanes = lax.broadcasted_iota(jnp.int32, (CH, 2 * P_SIZE), 1) < P_SIZE
    for pair in range(HB // 2):
        lanes = pl.ds(pair * 2 * P_SIZE, 2 * P_SIZE)
        v_pair = v_ref[:, lanes]
        both = []
        for h in (2 * pair, 2 * pair + 1):
            decay = jnp.exp(cum_cols[:, h : h + 1] - cum_rows[h : h + 1, :] + bias_ref[...])
            mixing = (scores_ref[...] * decay * step_rows[h : h + 1, :]).astype(bf16)
            both.append(jnp.dot(mixing, v_pair, preferred_element_type=f32))
        y_ref[:, lanes] = (
            jnp.where(low_lanes, both[0], both[1]) + skip_ref[:, lanes] * v_pair.astype(f32)
        )


def span_outputs(cum_t, step_t, seg_row, seg_col, b_rows, c_rows, values, skip_row):
    rows, width = values.shape
    wide = HB * P_SIZE
    return pl.pallas_call(
        span_kernel,
        grid=(rows // CH, width // wide),
        in_specs=[
            pl.BlockSpec((HB, CH), lambda s, g: (g, s)),
            pl.BlockSpec((HB, CH), lambda s, g: (g, s)),
            pl.BlockSpec((1, CH), lambda s, g: (0, s)),
            pl.BlockSpec((CH, 1), lambda s, g: (s, 0)),
            pl.BlockSpec((CH, N), lambda s, g: (s, 0)),
            pl.BlockSpec((CH, N), lambda s, g: (s, 0)),
            pl.BlockSpec((CH, wide), lambda s, g: (s, g)),
            pl.BlockSpec((1, wide), lambda s, g: (0, g)),
        ],
        out_specs=pl.BlockSpec((CH, wide), lambda s, g: (s, g)),
        out_shape=jax.ShapeDtypeStruct((rows, width), f32),
        scratch_shapes=[pltpu.VMEM((CH, CH), f32), pltpu.VMEM((CH, CH), f32)],
        name="span_outputs",
    )(cum_t, step_t, seg_row, seg_col, b_rows, c_rows, values, skip_row)


def span_back_kernel(cum_ref, step_ref, seg_row_ref, seg_col_ref, b_ref, c_ref, v_ref, skip_ref, g_ref,
                     dv_ref, dstep_ref, dcum_ref, db_ref, dc_ref, scores_ref, bias_ref, total_ref):
    @pl.when(pl.program_id(1) == 0)
    def _():
        scores_ref[...] = inner_product(c_ref[...], b_ref[...])
        bias_ref[...] = masked_bias(seg_row_ref[...], seg_col_ref[...])
        total_ref[...] = jnp.zeros_like(total_ref)

    cum_rows = cum_ref[...]
    cum_cols = cum_rows.T
    step_rows = step_ref[...]
    lane = lax.broadcasted_iota(jnp.int32, (CH, 2 * P_SIZE), 1)
    low_lanes = lane < P_SIZE
    row_sums = jnp.zeros((CH, 2 * P_SIZE), f32)
    zero = jnp.zeros((), bf16)
    for pair in range(HB // 2):
        lanes = pl.ds(pair * 2 * P_SIZE, 2 * P_SIZE)
        v_pair = v_ref[:, lanes]
        g_pair = g_ref[:, lanes]
        both = []
        for h in (2 * pair, 2 * pair + 1):
            step_row = step_rows[h : h + 1, :]
            scores = scores_ref[...]
            decay = jnp.exp(cum_cols[:, h : h + 1] - cum_rows[h : h + 1, :] + bias_ref[...])
            mixing_f = decay * step_row
            mixing = (scores * decay * step_row).astype(bf16)
            own = low_lanes if h % 2 == 0 else jnp.logical_not(low_lanes)
            d_mix = inner_product(jnp.where(own, g_pair, zero), v_pair)
            both.append(
                lax.dot_general(mixing, g_pair, (((0,), (0,)), ((), ())), preferred_element_type=f32)
            )
            total_ref[...] += d_mix * mixing_f
            weighted = d_mix * scores * decay
            column = jnp.sum(weighted, 0, keepdims=True)
            dstep_ref[h : h + 1, :] = column
            dcum_ref[h : h + 1, :] = -column * step_row
            row_sums = row_sums + jnp.where(
                lane == h, jnp.sum(weighted * step_row, 1, keepdims=True), 0.0
            )
        dv_ref[:, lanes] = (
            jnp.where(low_lanes, both[0], both[1]) + skip_ref[:, lanes] * g_pair.astype(f32)
        )
    dcum_ref[...] += row_sums.T[:HB, :]

    @pl.when(pl.program_id(1) == pl.num_programs(1) - 1)
    def _():
        total = total_ref[...]
        dc_ref[...] = jnp.dot(total, b_ref[...].astype(f32), precision=highest)
        db_ref[...] = jnp.dot(total.T, c_ref[...].astype(f32), precision=highest)


def span_backs(cum_t, step_t, seg_row, seg_col, b_rows, c_rows, values, skip_row, grads):
    rows, width = values.shape
    wide = HB * P_SIZE
    heads = width // P_SIZE
    return pl.pallas_call(
        span_back_kernel,
        grid=(rows // CH, width // wide),
        in_specs=[
            pl.BlockSpec((HB, CH), lambda s, g: (g, s)),
            pl.BlockSpec((HB, CH), lambda s, g: (g, s)),
            pl.BlockSpec((1, CH), lambda s, g: (0, s)),
            pl.BlockSpec((CH, 1), lambda s, g: (s, 0)),
            pl.BlockSpec((CH, N), lambda s, g: (s, 0)),
            pl.BlockSpec((CH, N), lambda s, g: (s, 0)),
            pl.BlockSpec((CH, wide), lambda s, g: (s, g)),
            pl.BlockSpec((1, wide), lambda s, g: (0, g)),
            pl.BlockSpec((CH, wide), lambda s, g: (s, g)),
        ],
        out_specs=[
            pl.BlockSpec((CH, wide), lambda s, g: (s, g)),
            pl.BlockSpec((HB, CH), lambda s, g: (g, s)),
            pl.BlockSpec((HB, CH), lambda s, g: (g, s)),
            pl.BlockSpec((CH, N), lambda s, g: (s, 0)),
            pl.BlockSpec((CH, N), lambda s, g: (s, 0)),
        ],
        out_shape=[
            jax.ShapeDtypeStruct((rows, width), f32),
            jax.ShapeDtypeStruct((heads, rows), f32),
            jax.ShapeDtypeStruct((heads, rows), f32),
            jax.ShapeDtypeStruct((rows, N), f32),
            jax.ShapeDtypeStruct((rows, N), f32),
        ],
        scratch_shapes=[pltpu.VMEM((CH, CH), f32)] * 3,
        name="span_backs",
    )(cum_t, step_t, seg_row, seg_col, b_rows, c_rows, values, skip_row, grads)


def shards(
    tokens,
    cotangent,
    seg_ids,
    carry_flags,
    inner_weight,
    inner_velocity,
    inner_average,
    groups_weight,
    groups_velocity,
    groups_average,
    stepper_weight,
    stepper_velocity,
    stepper_average,
    outer_weight,
    outer_velocity,
    outer_average,
    filters_weight,
    filters_velocity,
    filters_average,
    probes_weight,
    probes_velocity,
    probes_average,
    prenorm_weight,
    prenorm_velocity,
    prenorm_average,
    postnorm_weight,
    postnorm_velocity,
    postnorm_average,
    heads_weight,
    heads_velocity,
    heads_average,
):
    local_rows = tokens.shape[0]
    share = tokens.shape[1]
    value_width = filters_weight.shape[1]
    group_width = probes_weight.shape[1]
    heads_local = heads_weight.shape[1]
    span_count = local_rows // CH
    edge_count = KC - 1
    conv_width = value_width + group_width
    pad_heads = group_width - heads_local
    upper = lax.axis_index("head") == 1
    seq_count = lax.axis_size("seq")

    shard_a = jnp.concatenate(
        [
            inner_weight[:, 1],
            groups_weight,
            jnp.pad(stepper_weight, ((0, 0), (0, pad_heads))),
        ],
        1,
    ).astype(bf16)
    cut = shard_a.shape[1] // 2
    full_a = gather_two(shard_a, "seq")
    full_b = gather_two(inner_weight[:, 0].astype(bf16), "seq")
    full_c = gather_two(outer_weight.astype(bf16).T, "seq")

    rows_in = side_by_side(tokens, swap(tokens, "head", 1), upper)
    grads_in = side_by_side(cotangent, swap(cotangent, "head", 1), upper)
    rows_float = rows_in.astype(f32)
    inverse = lax.rsqrt(jnp.mean(rows_float * rows_float, -1, keepdims=True) + epsilon)
    unit_rows = rows_float * inverse
    normed = (unit_rows * prenorm_weight).astype(bf16)

    raw_a = jnp.concatenate(
        [jnp.dot(normed, w, preferred_element_type=f32) for w in full_a], 1
    )
    step_raw = raw_a[:, conv_width : conv_width + heads_local]
    conv_in = raw_a[:, :conv_width].astype(bf16)
    edge_rows = shifted(conv_in[local_rows - edge_count :], "seq", 1)
    extended = jnp.concatenate([edge_rows, conv_in], 0).astype(f32)
    masks = tap_masks(seg_ids, carry_flags, CH, KC)
    tap_rows = jnp.concatenate([filters_weight, probes_weight], 1)
    conv_out = conv_apply(extended, tap_rows, masks, KC)
    activated = jax.nn.silu(conv_out).astype(bf16)
    values = activated[:, :value_width]
    own_group = activated[:, value_width:]
    other_group = swap(own_group, "head", 1)
    b_rows = jnp.where(upper, other_group, own_group)
    c_rows = jnp.where(upper, own_group, other_group)

    step_pre = step_raw + heads_weight[0]
    step_size = jax.nn.softplus(step_pre)
    decay_rate = -jnp.exp(heads_weight[1])
    log_decay = step_size * decay_rate
    skip_row = expand(heads_weight[2:3])
    seg_spans = seg_ids.reshape(span_count, CH)
    cumulative, entering, leaving, chained = span_edges(
        log_decay.reshape(span_count, CH, heads_local), seg_spans, carry_flags
    )
    cum_t = cumulative.reshape(local_rows, heads_local).T
    step_t = step_size.T
    seg_row = seg_ids.reshape(1, local_rows)
    seg_col = seg_ids.reshape(local_rows, 1)
    enter_wide = expand(entering.reshape(local_rows, heads_local))
    leave_w = leaving.reshape(local_rows, heads_local) * step_size
    leave_wide = expand(leave_w)
    chain_wide = expand(chained)
    factor = jnp.prod(chained, 0)
    factor_wide = jnp.prod(chain_wide, 0)[None, None]
    factors = lax.all_to_all(
        jnp.broadcast_to(factor_wide, (seq_count, 1, value_width)), "seq", 0, 0
    )

    b_float = b_rows.astype(f32)
    c_float = c_rows.astype(f32)
    b_spans = b_float.reshape(span_count, CH, N)
    c_spans = c_float.reshape(span_count, CH, N)

    def by_span(array):
        return array.reshape((span_count, CH) + array.shape[1:])

    values_float = values.astype(f32)
    local_states = jnp.einsum(
        "cjn,cjw->cnw", b_spans, by_span(values_float * leave_wide), precision=highest
    )
    summary = local_states[0]
    for span in range(1, span_count):
        summary = chain_wide[span] * summary + local_states[span]
    state_list = [carried_in(summary, factors, "seq", False)]
    for span in range(span_count - 1):
        state_list.append(chain_wide[span] * state_list[-1] + local_states[span])
    entry_states = jnp.stack(state_list)

    local_out = span_outputs(
        cum_t, step_t, seg_row, seg_col, b_rows, c_rows, values, skip_row
    )
    c_state = jnp.einsum("cin,cnw->ciw", c_spans, entry_states, precision=highest).reshape(
        local_rows, value_width
    )
    ssd_out = local_out + enter_wide * c_state

    gate_pre = jnp.concatenate(
        [jnp.dot(normed, w, preferred_element_type=f32) for w in full_b], 1
    )
    gate_act = jax.nn.silu(gate_pre)
    gated = ssd_out * gate_act
    square_own = jnp.sum(gated * gated, -1)
    square_sum = square_own + swap(square_own, "head", 1)
    scale = lax.rsqrt(square_sum / DI + epsilon)[:, None]
    mixed = (gated * scale * postnorm_weight).astype(bf16)

    half_c = value_width // 2
    d_mixed = jnp.concatenate(
        [jnp.dot(grads_in, w, preferred_element_type=f32) for w in full_c], 1
    )
    d_scaled = d_mixed * postnorm_weight
    dot_own = jnp.sum(d_scaled * gated, -1)
    row_dot = dot_own + swap(dot_own, "head", 1)
    d_gated = scale * d_scaled - gated * scale**3 * (row_dot / DI)[:, None]
    d_ssd = (d_gated * gate_act).astype(bf16)
    d_gate = (d_gated * ssd_out * silu_slope(gate_pre)).astype(bf16)
    d_post = jnp.sum(d_mixed * gated * scale, 0)

    def outgoing(one, two):
        return one + swap(two, "head", 1)

    def split_features(array):
        lower_half, upper_half = array[:, :share], array[:, share:]
        return (
            jnp.where(upper, upper_half, lower_half),
            jnp.where(upper, lower_half, upper_half),
        )

    partial_out = sum(
        lax.dot_general(
            mixed[:, k * half_c : (k + 1) * half_c],
            full_c[k],
            (((1,), (1,)), ((), ())),
            preferred_element_type=f32,
        )
        for k in range(2)
    )
    projected = outgoing(*split_features(partial_out))
    output = (tokens.astype(f32) + projected).astype(bf16)

    def token_product(left, right):
        return lax.dot_general(left, right, (((0,), (0,)), ((), ())), preferred_element_type=f32)

    outer_grad = scatter_two(
        token_product(grads_in, mixed[:, :half_c]),
        token_product(grads_in, mixed[:, half_c:]),
        "seq",
    ).T
    gate_grad = scatter_two(
        token_product(normed, d_gate[:, :half_c]),
        token_product(normed, d_gate[:, half_c:]),
        "seq",
    )

    d_ssd_float = d_ssd.astype(f32)
    enter_grad = enter_wide * d_ssd_float
    pulls = jnp.einsum("cin,ciw->cnw", c_spans, by_span(enter_grad), precision=highest)
    pull_total = pulls[span_count - 1]
    for span in reversed(range(span_count - 1)):
        pull_total = chain_wide[span] * pull_total + pulls[span]
    next_list = [None] * span_count
    running = carried_in(pull_total, factors, "seq", True)
    for span in reversed(range(span_count)):
        next_list[span] = running
        if span > 0:
            running = chain_wide[span] * running + pulls[span]
    next_grads = jnp.stack(next_list)

    dv_local, d_step_t, d_cum_t, db_local, dc_local = span_backs(
        cum_t, step_t, seg_row, seg_col, b_rows, c_rows, values, skip_row, d_ssd
    )
    b_pull = jnp.einsum("cjn,cnw->cjw", b_spans, next_grads, precision=highest).reshape(
        local_rows, value_width
    )
    d_values = dv_local + leave_wide * b_pull
    d_leave = head_sums(values_float * b_pull)
    d_enter = head_sums(d_ssd_float * c_state)
    d_skip = head_sums(jnp.sum(d_ssd_float * values_float, 0, keepdims=True))[0]
    d_b_rows = db_local + jnp.einsum(
        "cjw,cnw->cjn", by_span(values_float * leave_wide), next_grads, precision=highest
    ).reshape(local_rows, N)
    d_c_rows = dc_local + jnp.einsum(
        "ciw,cnw->cin", by_span(enter_grad), entry_states, precision=highest
    ).reshape(local_rows, N)
    d_chain = head_sums(jnp.sum(next_grads * entry_states, 1))
    leave_rows = leaving.reshape(local_rows, heads_local)
    d_step = d_step_t.T + d_leave * leave_rows
    pull_terms = d_leave * leave_w
    d_cumul = by_span(
        d_cum_t.T - pull_terms + d_enter * entering.reshape(local_rows, heads_local)
    )
    last_term = jnp.sum(by_span(pull_terms), 1) + d_chain * chained
    at_or_after = (jnp.arange(CH)[:, None] <= jnp.arange(CH)[None, :]).astype(f32)
    d_log = (
        jnp.einsum("ki,cih->ckh", at_or_after, d_cumul, precision=highest) + last_term[:, None, :]
    ).reshape(local_rows, heads_local)
    d_step_all = d_step + d_log * decay_rate
    d_alog = jnp.sum(d_log * step_size, 0) * decay_rate
    d_pre = d_step_all * jax.nn.sigmoid(step_pre)
    d_bias = jnp.sum(d_pre, 0)
    d_step_low = d_pre.astype(bf16)

    group_share = jnp.where(upper, d_c_rows, d_b_rows) + swap(
        jnp.where(upper, d_b_rows, d_c_rows), "head", 1
    )
    d_conv = jnp.concatenate([d_values, group_share], 1) * silu_slope(conv_out)
    d_taps, ext_grad = conv_backward(extended, tap_rows, masks, d_conv, KC)
    from_next = shifted(ext_grad[:edge_count], "seq", -1)
    d_conv_in = ext_grad[edge_count:] + jnp.pad(from_next, ((local_rows - edge_count, 0), (0, 0)))
    grads_a = jnp.concatenate(
        [d_conv_in.astype(bf16), jnp.pad(d_step_low, ((0, 0), (0, pad_heads)))], 1
    )
    rest_grad = scatter_two(
        token_product(normed, grads_a[:, :cut]),
        token_product(normed, grads_a[:, cut:]),
        "seq",
    )

    def back_product(grads, weights):
        width = weights[0].shape[1]
        return sum(
            lax.dot_general(
                grads[:, k * width : (k + 1) * width],
                weights[k],
                (((1,), (1,)), ((), ())),
                preferred_element_type=f32,
            )
            for k in range(2)
        )

    d_normed_part = back_product(d_gate, full_b) + back_product(grads_a, full_a)
    d_normed = outgoing(*split_features(d_normed_part))
    own_unit = jnp.where(upper, unit_rows[:, share:], unit_rows[:, :share])
    own_gain = jnp.where(upper, prenorm_weight[share:], prenorm_weight[:share])
    own_rows = tokens.astype(f32)
    d_prenorm = jnp.sum(d_normed * own_unit, 0)
    d_unit_in = d_normed * own_gain
    mean_own = jnp.sum(d_unit_in * own_rows, -1)
    row_mean = ((mean_own + swap(mean_own, "head", 1)) / D)[:, None]
    input_gradient = (
        cotangent.astype(f32) + inverse * d_unit_in - own_rows * inverse**3 * row_mean
    )

    heads_flat = jnp.concatenate([d_bias, d_alog, d_skip])
    small = jnp.concatenate(
        [
            d_taps,
            jnp.pad(d_post, (0, group_width))[None],
            jnp.pad(jnp.concatenate([d_prenorm, heads_flat]), (0, conv_width - share - 3 * heads_local))[None],
        ],
        0,
    )
    small = butterfly_sum(small, "seq")
    filters_grad = small[: KC + 1, :value_width]
    probes_grad = small[: KC + 1, value_width:]
    postnorm_grad = small[KC + 1, :value_width]
    prenorm_own = small[KC + 2 : KC + 3, :share]
    prenorm_grad = side_by_side(prenorm_own, swap(prenorm_own, "head", 1), upper)[0]
    heads_grad = small[KC + 2, share : share + 3 * heads_local].reshape(3, heads_local)

    inner_grad = jnp.stack([gate_grad, rest_grad[:, :value_width]], 1)
    groups_grad = rest_grad[:, value_width:conv_width]
    stepper_grad = rest_grad[:, conv_width : conv_width + heads_local]
    root = math.sqrt(local_rows * seq_count)
    inner_new = apply_update(
        inner_weight, inner_velocity, inner_average, inner_grad, D ** (-0.5) / root
    )
    groups_new = apply_update(
        groups_weight, groups_velocity, groups_average, groups_grad, D ** (-0.5) / root
    )
    stepper_new = apply_update(
        stepper_weight, stepper_velocity, stepper_average, stepper_grad, (4 * D) ** (-0.5) / root
    )
    outer_new = apply_update(
        outer_weight, outer_velocity, outer_average, outer_grad, DI ** (-0.5) / root
    )
    filters_new = apply_update(
        filters_weight, filters_velocity, filters_average, filters_grad, 0.5 / root
    )
    probes_new = apply_update(
        probes_weight, probes_velocity, probes_average, probes_grad, 0.5 / root
    )
    prenorm_new = apply_update(
        prenorm_weight, prenorm_velocity, prenorm_average, prenorm_grad, 0.1 / root
    )
    postnorm_new = apply_update(
        postnorm_weight, postnorm_velocity, postnorm_average, postnorm_grad, 0.1 / root
    )
    heads_new = apply_update(heads_weight, heads_velocity, heads_average, heads_grad, 0.5 / root)
    return (
        output,
        input_gradient,
        inner_new[0],
        inner_new[1],
        inner_new[2],
        inner_new[3],
        groups_new[0],
        groups_new[1],
        groups_new[2],
        groups_new[3],
        stepper_new[0],
        stepper_new[1],
        stepper_new[2],
        stepper_new[3],
        outer_new[0],
        outer_new[1],
        outer_new[2],
        outer_new[3],
        filters_new[0],
        filters_new[1],
        filters_new[2],
        filters_new[3],
        probes_new[0],
        probes_new[1],
        probes_new[2],
        probes_new[3],
        prenorm_new[0],
        prenorm_new[1],
        prenorm_new[2],
        prenorm_new[3],
        postnorm_new[0],
        postnorm_new[1],
        postnorm_new[2],
        postnorm_new[3],
        heads_new[0],
        heads_new[1],
        heads_new[2],
        heads_new[3],
    )


def solution(mesh):
    return jax.shard_map(
        shards,
        mesh=mesh,
        in_specs=(
            P("seq", "head"),
            P("seq", "head"),
            P("seq"),
            P("seq"),
            P("seq", None, "head"),
            P("seq", None, "head"),
            P("seq", None, "head"),
            P("seq", "head"),
            P("seq", "head"),
            P("seq", "head"),
            P("seq", "head"),
            P("seq", "head"),
            P("seq", "head"),
            P("head", "seq"),
            P("head", "seq"),
            P("head", "seq"),
            P(None, "head"),
            P(None, "head"),
            P(None, "head"),
            P(None, "head"),
            P(None, "head"),
            P(None, "head"),
            P(),
            P(),
            P(),
            P("head"),
            P("head"),
            P("head"),
            P(None, "head"),
            P(None, "head"),
            P(None, "head"),
        ),
        out_specs=(
            P("seq", "head"),
            P("seq", "head"),
            P("seq", None, "head"),
            P("seq", None, "head"),
            P("seq", None, "head"),
            P("seq", None, "head"),
            P("seq", "head"),
            P("seq", "head"),
            P("seq", "head"),
            P("seq", "head"),
            P("seq", "head"),
            P("seq", "head"),
            P("seq", "head"),
            P("seq", "head"),
            P("head", "seq"),
            P("head", "seq"),
            P("head", "seq"),
            P("head", "seq"),
            P(None, "head"),
            P(None, "head"),
            P(None, "head"),
            P(None, "head"),
            P(None, "head"),
            P(None, "head"),
            P(None, "head"),
            P(None, "head"),
            P(),
            P(),
            P(),
            P(),
            P("head"),
            P("head"),
            P("head"),
            P("head"),
            P(None, "head"),
            P(None, "head"),
            P(None, "head"),
            P(None, "head"),
        ),
        check_vma=False,
    )
```

```python
import math

import jax
import jax.numpy as jnp
from jax import lax
from jax.experimental import pallas as pl
from jax.experimental.pallas import tpu as pltpu
from jax.sharding import PartitionSpec as P


D = 1536
DI = 3072
P_SIZE = 64
N = 128
KC = 4
CH = 256
HB = 8
SEQ = "seq"
HEAD = "head"


epsilon = 1e-05
momentum_decay = 0.9
average_decay = 0.9
highest = lax.Precision.HIGHEST
f32 = jnp.float32
bf16 = jnp.bfloat16


def shifted(array, axis, by):
    count = lax.axis_size(axis)
    pairs = [(i, i + by) for i in range(count) if 0 <= i + by < count]
    return lax.ppermute(array, axis, pairs)


def swap(array, axis, mask):
    count = lax.axis_size(axis)
    return lax.ppermute(array, axis, [(i, i ^ mask) for i in range(count)])


def bit_orders(axis):
    bits = lax.axis_size(axis).bit_length() - 1
    first = list(range(bits))
    second = first[:]
    if bits > 1:
        second[0], second[1] = 1, 0
    return first, second


def after(values, *others):
    return lax.optimization_barrier((values, others))[0]


def assemble(own, other, axis, bit, done):
    upper = ((lax.axis_index(axis) >> bit) & 1) == 1
    before = 1 << sum(1 for b in done if b > bit)
    split = (before, own.shape[0] // before, own.shape[1])
    own, other = own.reshape(split), other.reshape(split)
    return jnp.stack([jnp.where(upper, other, own), jnp.where(upper, own, other)], 1).reshape(
        2 * split[0] * split[1], split[2]
    )


def gather_rows(held, axis, bits, done=()):
    done = list(done)
    for bit in bits:
        held = assemble(held, swap(held, axis, 1 << bit), axis, bit, done)
        done.append(bit)
    return held


def sides_of(held, axis, bit, left):
    mine = (lax.axis_index(axis) >> bit) & 1
    before = 1 << sum(1 for b in left if b > bit)
    split = held.reshape(before, 2, held.shape[0] // (2 * before), held.shape[1])
    flat = (held.shape[0] // 2, held.shape[1])
    kept = lax.dynamic_index_in_dim(split, mine, 1, False).reshape(flat)
    return kept, lax.dynamic_index_in_dim(split, 1 - mine, 1, False).astype(bf16).reshape(flat)


def scatter_rows(held, axis, bits, left):
    left = list(left)
    for bit in bits:
        kept, sent = sides_of(held, axis, bit, left)
        held = kept + swap(sent, axis, 1 << bit).astype(f32)
        left.remove(bit)
    return held


def pick_columns(array, axis, bit, other):
    mine = (lax.axis_index(axis) >> bit) & 1
    run = (array.shape[1] // lax.axis_size(axis)) << bit
    split = array.reshape(array.shape[0], array.shape[1] // (2 * run), 2, run)
    return lax.dynamic_index_in_dim(split, 1 - mine if other else mine, 2, False).reshape(
        array.shape[0], array.shape[1] // 2
    )


def token_product(left, right):
    return lax.dot_general(left, right, (((0,), (0,)), ((), ())), preferred_element_type=f32)


def butterfly_sum(array, axis, bits):
    for bit in bits:
        array = array + swap(array, axis, 1 << bit)
    return array


def side_by_side(own, other, upper):
    return jnp.concatenate([jnp.where(upper, other, own), jnp.where(upper, own, other)], 1)


def expand(array):
    count = array.shape[-1]
    spread = (
        jnp.arange(count)[:, None] == (jnp.arange(count * P_SIZE) // P_SIZE)[None, :]
    ).astype(f32)
    return jnp.dot(array, spread, precision=highest)


def silu_slope(values):
    sigmoid = jax.nn.sigmoid(values)
    return sigmoid * (1.0 + values * (1.0 - sigmoid))


def tap_masks(seg_rows, flag_rows, span_len, taps):
    number = seg_rows.shape[0]
    within = jnp.arange(number) % span_len
    first_seg = jnp.repeat(seg_rows[::span_len], span_len)
    continued = (jnp.repeat(flag_rows, span_len) == 1) & (seg_rows == first_seg)
    stacked = []
    for lagged in range(1, taps):
        earlier = jnp.concatenate([jnp.full((lagged,), -1, jnp.int32), seg_rows[:-lagged]])
        stacked.append(jnp.where(within >= lagged, earlier == seg_rows, continued))
    return jnp.stack(stacked).astype(jnp.float32)


def conv_apply(extended, tap_rows, masks, taps):
    number = extended.shape[0] - (taps - 1)
    total = tap_rows[taps] + tap_rows[0] * extended[taps - 1 :]
    for lagged in range(1, taps):
        begin = taps - 1 - lagged
        total = (
            total + tap_rows[lagged] * masks[lagged - 1][:, None] * extended[begin : begin + number]
        )
    return total


def conv_backward(extended, tap_rows, masks, grads, taps):
    number = grads.shape[0]
    tap_grads = [jnp.sum(grads * extended[taps - 1 :], 0)]
    ext_grad = jnp.pad(tap_rows[0] * grads, ((taps - 1, 0), (0, 0)))
    for lagged in range(1, taps):
        masked = masks[lagged - 1][:, None] * grads
        begin = taps - 1 - lagged
        tap_grads.append(jnp.sum(masked * extended[begin : begin + number], 0))
        ext_grad = ext_grad + jnp.pad(tap_rows[lagged] * masked, ((begin, lagged), (0, 0)))
    tap_grads.append(jnp.sum(grads, 0))
    return (jnp.stack(tap_grads), ext_grad)


def span_edges(log_decay, seg_spans, flag_spans):
    length = log_decay.shape[1]
    lower = (jnp.arange(length)[:, None] >= jnp.arange(length)[None, :]).astype(f32)
    cumulative = jnp.einsum("ij,cjh->cih", lower, log_decay, precision=highest)
    carried = flag_spans.astype(jnp.float32)[:, None] * (seg_spans == seg_spans[:, :1]).astype(
        jnp.float32
    )
    keeping = (seg_spans == seg_spans[:, -1:]).astype(jnp.float32)
    entering = carried[:, :, None] * jnp.exp(cumulative)
    leaving = keeping[:, :, None] * jnp.exp(cumulative[:, -1:, :] - cumulative)
    chained = carried[:, -1:] * jnp.exp(cumulative[:, -1, :])
    return (cumulative, entering, leaving, chained)


def apply_update(master, velocity, average, gradient, rate_value):
    moment = momentum_decay * velocity + gradient
    stepped = master - rate_value * (gradient + momentum_decay * moment)
    smoothed = average_decay * average + (1.0 - average_decay) * stepped
    return (gradient, stepped, moment, smoothed)


def walk_kernel(count, reverse, part_ref, factor_ref, out_ref):
    def one(turn, state):
        source = count - 1 - turn if reverse else turn
        out_ref[source] = state
        return factor_ref[source] * state + part_ref[source, :, : state.shape[1]]

    lax.fori_loop(0, count, one, jnp.zeros(out_ref.shape[1:], f32))


def parts_out(part, axis):
    count = lax.axis_size(axis)
    pieces = part.reshape((count, part.shape[0] // count) + part.shape[1:])
    return lax.all_to_all(pieces, axis, 0, 0)


def walked_in(pieces, factors, axis, reverse):
    count = lax.axis_size(axis)
    rows, width = pieces.shape[1], factors.shape[2]
    walked = pl.pallas_call(
        lambda *refs: walk_kernel(count, reverse, *refs),
        out_shape=jax.ShapeDtypeStruct((count, rows, width), f32),
        name="walk",
    )(pieces, factors)
    back = lax.all_to_all(walked, axis, 0, 0)
    return walked, back.reshape(count * rows, width)


def update_kernel(rate_value, gate_ref, rest_ref, w_ref, v_ref, a_ref, g_out, w_out, v_out, a_out):
    for k, grad_ref in ((0, gate_ref), (1, rest_ref)):
        grad = grad_ref[...]
        moment = momentum_decay * v_ref[:, k, :] + grad
        stepped = w_ref[:, k, :] - rate_value * (grad + momentum_decay * moment)
        g_out[:, k, :] = grad
        w_out[:, k, :] = stepped
        v_out[:, k, :] = moment
        a_out[:, k, :] = average_decay * a_ref[:, k, :] + (1.0 - average_decay) * stepped


def update_inner(weight, velocity, average, gate_grad, rest_grad, rate_value):
    rows, two, width = weight.shape
    step = 32 if rows % 32 == 0 else rows
    flat = pl.BlockSpec((step, width), lambda r: (r, 0))
    deep = pl.BlockSpec((step, two, width), lambda r: (r, 0, 0))
    return pl.pallas_call(
        lambda *refs: update_kernel(rate_value, *refs),
        grid=(rows // step,),
        in_specs=[flat, flat, deep, deep, deep],
        out_specs=[deep] * 4,
        out_shape=[jax.ShapeDtypeStruct(weight.shape, f32)] * 4,
        name="update_inner",
    )(gate_grad, rest_grad, weight, velocity, average)


def masked_bias(seg_row, seg_col):
    length = seg_row.shape[1]
    rows = lax.broadcasted_iota(jnp.int32, (length, length), 0)
    cols = lax.broadcasted_iota(jnp.int32, (length, length), 1)
    return jnp.where((rows >= cols) & (seg_col == seg_row), 0.0, -1e30).astype(f32)


def inner_product(one, two):
    return lax.dot_general(one, two, (((1,), (1,)), ((), ())), preferred_element_type=f32)


def halves_of(array):
    high = array.astype(bf16)
    return high, (array - high.astype(f32)).astype(bf16)


def exact_dot(left, right, contract=((1,), (0,))):
    return sum(
        lax.dot_general(left, part, (contract, ((), ())), preferred_element_type=f32)
        for part in halves_of(right)
    )


def pair_columns(columns, pair, low_lanes):
    return jnp.where(
        low_lanes, columns[:, 2 * pair : 2 * pair + 1], columns[:, 2 * pair + 1 : 2 * pair + 2]
    )


def entry_state(first_ref, added_ref, chain_ref, lanes):
    first = first_ref[:, lanes]
    return jnp.where(
        pl.program_id(0) == 0, first, chain_ref[:, lanes] * first + added_ref[:, lanes]
    )


def gated_pieces(refs, pair, low_lanes, enter):
    local_ref, gate_ref, mixed_ref, c_ref, first_ref, added_ref, chain_ref, gain_ref = refs
    lanes = pl.ds(pair * 2 * P_SIZE, 2 * P_SIZE)
    enter_pair = pair_columns(enter, pair, low_lanes)
    states = entry_state(first_ref, added_ref, chain_ref, lanes)
    out = local_ref[:, lanes] + enter_pair * exact_dot(c_ref[...], states)
    gate = gate_ref[:, lanes]
    sigmoid = 1.0 / (1.0 + jnp.exp(-gate))
    act = gate * sigmoid
    return out, gate, sigmoid, act, out * act, mixed_ref[:, lanes], gain_ref[:, lanes], enter_pair


def row_sums_kernel(*refs):
    refs, (enter_ref, out_ref) = refs[:8], refs[8:]
    enter = enter_ref[...]
    lane = lax.broadcasted_iota(jnp.int32, (CH, 2 * P_SIZE), 1)
    squares = jnp.zeros((CH, 2 * P_SIZE), f32)
    dots = jnp.zeros((CH, 2 * P_SIZE), f32)
    for pair in range(refs[0].shape[1] // (2 * P_SIZE)):
        gated, d_mixed, gain = gated_pieces(refs, pair, lane < P_SIZE, enter)[4:7]
        squares = squares + gated * gated
        dots = dots + d_mixed * gain * gated
    out_ref[...] = jnp.where(
        lane == 0,
        jnp.sum(squares, 1, keepdims=True),
        jnp.where(lane == 1, jnp.sum(dots, 1, keepdims=True), 0.0),
    )


def middle_specs(width, heads):
    wide = pl.BlockSpec((CH, width), lambda s: (s, 0))
    state = pl.BlockSpec((N, width), lambda s: (0, 0))
    row = pl.BlockSpec((1, width), lambda s: (0, 0))
    group = pl.BlockSpec((CH, N), lambda s: (s, 0))
    return [wide, wide, wide, group, state, state, row, row, pl.BlockSpec((CH, heads), lambda s: (s, 0))]


def row_sums(*args):
    rows, width = args[0].shape
    return pl.pallas_call(
        row_sums_kernel,
        grid=(rows // CH,),
        in_specs=middle_specs(width, args[-1].shape[1]),
        out_specs=pl.BlockSpec((CH, 2 * P_SIZE), lambda s: (s, 0)),
        out_shape=jax.ShapeDtypeStruct((rows, 2 * P_SIZE), f32),
        name="row_sums",
    )(*args)


def middle_kernel(*all_refs):
    refs, (enter_ref, own_ref, other_ref) = all_refs[:8], all_refs[8:11]
    mixed_out, ssd_out, gate_out, post_out, total_out, last_out = all_refs[11:]
    c_ref, chain_ref = refs[3], refs[6]

    @pl.when(pl.program_id(0) == 0)
    def _():
        post_out[...] = jnp.zeros_like(post_out)
        total_out[...] = jnp.zeros_like(total_out)

    enter = enter_ref[...]
    both = own_ref[...] + other_ref[...]
    scale = lax.rsqrt(both[:, 0:1] / DI + epsilon)
    pulled = scale * scale * scale * (both[:, 1:2] / DI)
    low_lanes = lax.broadcasted_iota(jnp.int32, (CH, 2 * P_SIZE), 1) < P_SIZE
    for pair in range(refs[0].shape[1] // (2 * P_SIZE)):
        lanes = pl.ds(pair * 2 * P_SIZE, 2 * P_SIZE)
        out, gate, sigmoid, act, gated, d_mixed, gain, enter_pair = gated_pieces(
            refs, pair, low_lanes, enter
        )
        mixed_out[:, lanes] = (gated * scale * gain).astype(bf16)
        d_gated = scale * (d_mixed * gain) - gated * pulled
        d_ssd = (d_gated * act).astype(bf16)
        ssd_out[:, lanes] = d_ssd
        gate_out[:, lanes] = (d_gated * out * (sigmoid * (1.0 + gate * (1.0 - sigmoid)))).astype(bf16)
        post_out[:, lanes] += jnp.sum(d_mixed * gated * scale, 0, keepdims=True)
        pull = exact_dot(c_ref[...], enter_pair * d_ssd.astype(f32), ((0,), (0,)))
        total_out[:, lanes] += jnp.where(pl.program_id(0) == 0, 1.0, chain_ref[:, lanes]) * pull
        last_out[:, lanes] = pull


def middle(*args):
    rows, width = args[0].shape
    wide = pl.BlockSpec((CH, width), lambda s: (s, 0))
    state = pl.BlockSpec((N, width), lambda s: (0, 0))
    low = jax.ShapeDtypeStruct((rows, width), bf16)
    return pl.pallas_call(
        middle_kernel,
        grid=(rows // CH,),
        in_specs=middle_specs(width, args[-3].shape[1])
        + [pl.BlockSpec((CH, 2 * P_SIZE), lambda s: (s, 0))] * 2,
        out_specs=[wide, wide, wide, pl.BlockSpec((1, width), lambda s: (0, 0)), state, state],
        out_shape=[
            low,
            low,
            low,
            jax.ShapeDtypeStruct((1, width), f32),
            jax.ShapeDtypeStruct((N, width), f32),
            jax.ShapeDtypeStruct((N, width), f32),
        ],
        name="middle",
    )(*args)


def late_kernel(v_ref, g_ref, b_ref, c_ref, first_ref, added_ref, chain_first_ref, exit_ref, pull_ref,
                chain_last_ref, dv_ref, db_ref, dc_ref, dstep_ref, dcum_ref, enter_ref, leave_ref,
                step_ref, chain_ref, dv_out, db_out, dc_out, dstep_out, dlog_out, dskip_out):
    enter, leave, step = enter_ref[...], leave_ref[...], step_ref[...]
    heads = enter.shape[1]
    wide = 2 * P_SIZE
    lane = lax.broadcasted_iota(jnp.int32, (CH, wide), 1)
    low_lanes = lane < P_SIZE
    from_lane = lax.broadcasted_iota(jnp.int32, (wide, wide), 0)
    to_head = lax.broadcasted_iota(jnp.int32, (wide, wide), 1)
    leave_w = leave * step
    d_leave = jnp.zeros((CH, wide), f32)
    d_enter = jnp.zeros((CH, wide), f32)
    d_chain = jnp.zeros((8, wide), f32)
    d_skip = jnp.zeros((8, wide), f32)
    last_span = pl.program_id(0) == pl.num_programs(0) - 1
    d_b, d_c = db_ref[...], dc_ref[...]
    b_low, c_low = b_ref[...], c_ref[...]

    def summed(array, pick):
        high, rest = halves_of(array)
        return jnp.dot(high, pick, preferred_element_type=f32) + jnp.dot(
            rest, pick, preferred_element_type=f32
        )

    def crossed(one, two):
        one_high, one_rest = halves_of(one)
        two_high, two_rest = halves_of(two)
        return (
            inner_product(one_high, two_high)
            + inner_product(one_high, two_rest)
            + inner_product(one_rest, two_high)
        )

    for pair in range(heads // 2):
        lanes = pl.ds(pair * wide, wide)
        pick = (to_head == 2 * pair + from_lane // P_SIZE).astype(f32).astype(bf16)
        values = v_ref[:, lanes].astype(f32)
        grads = g_ref[:, lanes].astype(f32)
        states = entry_state(first_ref, added_ref, chain_first_ref, lanes)
        nexts = exit_ref[:, lanes]
        nexts = jnp.where(last_span, nexts, chain_last_ref[:, lanes] * nexts + pull_ref[:, lanes])
        leave_pair = pair_columns(leave_w, pair, low_lanes)
        b_pull = exact_dot(b_low, nexts)
        dv_out[:, lanes] = dv_ref[:, lanes] + leave_pair * b_pull
        d_leave = d_leave + summed(values * b_pull, pick)
        d_b = d_b + crossed(values * leave_pair, nexts)
        d_enter = d_enter + summed(grads * exact_dot(c_low, states), pick)
        d_c = d_c + crossed(pair_columns(enter, pair, low_lanes) * grads, states)
        column = jnp.sum(nexts * states, 0, keepdims=True)
        d_chain = d_chain + summed(jnp.broadcast_to(column, (8, wide)), pick)
        column = jnp.sum(grads * values, 0, keepdims=True)
        d_skip = d_skip + summed(jnp.broadcast_to(column, (8, wide)), pick)
    dskip_out[0] = d_skip
    db_out[...] = d_b
    dc_out[...] = d_c
    d_leave, d_enter, d_chain = d_leave[:, :heads], d_enter[:, :heads], d_chain[:1, :heads]
    dstep_out[...] = dstep_ref[...].T + d_leave * leave
    pulled = d_leave * leave_w
    d_cum = dcum_ref[...].T - pulled + d_enter * enter
    at_or_after = (
        lax.broadcasted_iota(jnp.int32, (CH, CH), 0) <= lax.broadcasted_iota(jnp.int32, (CH, CH), 1)
    ).astype(f32)
    last = jnp.sum(pulled, 0, keepdims=True) + d_chain * chain_ref[0]
    dlog_out[...] = jnp.dot(at_or_after, d_cum, precision=highest) + last


def late(values, grads, b_rows, c_rows, first, added, chain_first, last, pull, chain_last, dv, db, dc,
         d_step_t, d_cum_t, enter, leave, step, chained):
    rows, width = grads.shape
    heads = width // P_SIZE
    wide = pl.BlockSpec((CH, width), lambda s: (s, 0))
    group = pl.BlockSpec((CH, N), lambda s: (s, 0))
    state = pl.BlockSpec((N, width), lambda s: (0, 0))
    row = pl.BlockSpec((1, width), lambda s: (0, 0))
    turned = pl.BlockSpec((heads, CH), lambda s: (0, s))
    thin = pl.BlockSpec((CH, heads), lambda s: (s, 0))
    one = pl.BlockSpec((1, 1, heads), lambda s: (s, 0, 0))
    return pl.pallas_call(
        late_kernel,
        grid=(rows // CH,),
        in_specs=[wide, wide, group, group, state, state, row, state, state, row, wide, group, group,
                  turned, turned, thin, thin, thin, one],
        out_specs=[wide, group, group, thin, thin,
                   pl.BlockSpec((1, 8, 2 * P_SIZE), lambda s: (s, 0, 0))],
        out_shape=[
            jax.ShapeDtypeStruct((rows, width), f32),
            jax.ShapeDtypeStruct((rows, N), f32),
            jax.ShapeDtypeStruct((rows, N), f32),
            jax.ShapeDtypeStruct((rows, heads), f32),
            jax.ShapeDtypeStruct((rows, heads), f32),
            jax.ShapeDtypeStruct((rows // CH, 8, 2 * P_SIZE), f32),
        ],
        name="late",
    )(values, grads, b_rows, c_rows, first, added, chain_first, last, pull, chain_last, dv, db, dc,
      d_step_t, d_cum_t, enter, leave, step, chained[:, None])


def span_kernel(cum_ref, step_ref, seg_row_ref, seg_col_ref, b_ref, c_ref, v_ref, skip_ref, y_ref,
                scores_ref, bias_ref):
    @pl.when(pl.program_id(1) == 0)
    def _():
        scores_ref[...] = inner_product(c_ref[...], b_ref[...])
        bias_ref[...] = masked_bias(seg_row_ref[...], seg_col_ref[...])

    cum_rows = cum_ref[...]
    cum_cols = cum_rows.T
    step_rows = step_ref[...]
    low_lanes = lax.broadcasted_iota(jnp.int32, (CH, 2 * P_SIZE), 1) < P_SIZE
    for pair in range(HB // 2):
        lanes = pl.ds(pair * 2 * P_SIZE, 2 * P_SIZE)
        v_pair = v_ref[:, lanes]
        both = []
        for h in (2 * pair, 2 * pair + 1):
            decay = jnp.exp(cum_cols[:, h : h + 1] - cum_rows[h : h + 1, :] + bias_ref[...])
            mixing = (scores_ref[...] * decay * step_rows[h : h + 1, :]).astype(bf16)
            both.append(jnp.dot(mixing, v_pair, preferred_element_type=f32))
        y_ref[:, lanes] = (
            jnp.where(low_lanes, both[0], both[1]) + skip_ref[:, lanes] * v_pair.astype(f32)
        )


def span_outputs(cum_t, step_t, seg_row, seg_col, b_rows, c_rows, values, skip_row):
    rows, width = values.shape[0], skip_row.shape[1]
    wide = HB * P_SIZE
    return pl.pallas_call(
        span_kernel,
        grid=(rows // CH, width // wide),
        in_specs=[
            pl.BlockSpec((HB, CH), lambda s, g: (g, s)),
            pl.BlockSpec((HB, CH), lambda s, g: (g, s)),
            pl.BlockSpec((1, CH), lambda s, g: (0, s)),
            pl.BlockSpec((CH, 1), lambda s, g: (s, 0)),
            pl.BlockSpec((CH, N), lambda s, g: (s, 0)),
            pl.BlockSpec((CH, N), lambda s, g: (s, 0)),
            pl.BlockSpec((CH, wide), lambda s, g: (s, g)),
            pl.BlockSpec((1, wide), lambda s, g: (0, g)),
        ],
        out_specs=pl.BlockSpec((CH, wide), lambda s, g: (s, g)),
        out_shape=jax.ShapeDtypeStruct((rows, width), f32),
        scratch_shapes=[pltpu.VMEM((CH, CH), f32), pltpu.VMEM((CH, CH), f32)],
        name="span_outputs",
    )(cum_t, step_t, seg_row, seg_col, b_rows, c_rows, values, skip_row)


def span_back_kernel(cum_ref, step_ref, seg_row_ref, seg_col_ref, b_ref, c_ref, v_ref, skip_ref, g_ref,
                     dv_ref, dstep_ref, dcum_ref, db_ref, dc_ref, scores_ref, bias_ref, total_ref):
    @pl.when(pl.program_id(1) == 0)
    def _():
        scores_ref[...] = inner_product(c_ref[...], b_ref[...])
        bias_ref[...] = masked_bias(seg_row_ref[...], seg_col_ref[...])
        total_ref[...] = jnp.zeros_like(total_ref)

    cum_rows = cum_ref[...]
    cum_cols = cum_rows.T
    step_rows = step_ref[...]
    lane = lax.broadcasted_iota(jnp.int32, (CH, 2 * P_SIZE), 1)
    low_lanes = lane < P_SIZE
    row_sums = jnp.zeros((CH, 2 * P_SIZE), f32)
    zero = jnp.zeros((), bf16)
    for pair in range(HB // 2):
        lanes = pl.ds(pair * 2 * P_SIZE, 2 * P_SIZE)
        v_pair = v_ref[:, lanes]
        g_pair = g_ref[:, lanes]
        both = []
        for h in (2 * pair, 2 * pair + 1):
            step_row = step_rows[h : h + 1, :]
            scores = scores_ref[...]
            decay = jnp.exp(cum_cols[:, h : h + 1] - cum_rows[h : h + 1, :] + bias_ref[...])
            mixing_f = decay * step_row
            mixing = (scores * decay * step_row).astype(bf16)
            own = low_lanes if h % 2 == 0 else jnp.logical_not(low_lanes)
            d_mix = inner_product(jnp.where(own, g_pair, zero), v_pair)
            both.append(
                lax.dot_general(mixing, g_pair, (((0,), (0,)), ((), ())), preferred_element_type=f32)
            )
            total_ref[...] += d_mix * mixing_f
            weighted = d_mix * scores * decay
            column = jnp.sum(weighted, 0, keepdims=True)
            dstep_ref[h : h + 1, :] = column
            dcum_ref[h : h + 1, :] = -column * step_row
            row_sums = row_sums + jnp.where(
                lane == h, jnp.sum(weighted * step_row, 1, keepdims=True), 0.0
            )
        dv_ref[:, lanes] = (
            jnp.where(low_lanes, both[0], both[1]) + skip_ref[:, lanes] * g_pair.astype(f32)
        )
    dcum_ref[...] += row_sums.T[:HB, :]

    @pl.when(pl.program_id(1) == pl.num_programs(1) - 1)
    def _():
        total = total_ref[...]
        dc_ref[...] = jnp.dot(total, b_ref[...].astype(f32), precision=highest)
        db_ref[...] = jnp.dot(total.T, c_ref[...].astype(f32), precision=highest)


def span_backs(cum_t, step_t, seg_row, seg_col, b_rows, c_rows, values, skip_row, grads):
    rows, width = grads.shape
    wide = HB * P_SIZE
    heads = width // P_SIZE
    return pl.pallas_call(
        span_back_kernel,
        grid=(rows // CH, width // wide),
        in_specs=[
            pl.BlockSpec((HB, CH), lambda s, g: (g, s)),
            pl.BlockSpec((HB, CH), lambda s, g: (g, s)),
            pl.BlockSpec((1, CH), lambda s, g: (0, s)),
            pl.BlockSpec((CH, 1), lambda s, g: (s, 0)),
            pl.BlockSpec((CH, N), lambda s, g: (s, 0)),
            pl.BlockSpec((CH, N), lambda s, g: (s, 0)),
            pl.BlockSpec((CH, wide), lambda s, g: (s, g)),
            pl.BlockSpec((1, wide), lambda s, g: (0, g)),
            pl.BlockSpec((CH, wide), lambda s, g: (s, g)),
        ],
        out_specs=[
            pl.BlockSpec((CH, wide), lambda s, g: (s, g)),
            pl.BlockSpec((HB, CH), lambda s, g: (g, s)),
            pl.BlockSpec((HB, CH), lambda s, g: (g, s)),
            pl.BlockSpec((CH, N), lambda s, g: (s, 0)),
            pl.BlockSpec((CH, N), lambda s, g: (s, 0)),
        ],
        out_shape=[
            jax.ShapeDtypeStruct((rows, width), f32),
            jax.ShapeDtypeStruct((heads, rows), f32),
            jax.ShapeDtypeStruct((heads, rows), f32),
            jax.ShapeDtypeStruct((rows, N), f32),
            jax.ShapeDtypeStruct((rows, N), f32),
        ],
        scratch_shapes=[pltpu.VMEM((CH, CH), f32)] * 3,
        name="span_backs",
    )(cum_t, step_t, seg_row, seg_col, b_rows, c_rows, values, skip_row, grads)


def shards(
    tokens,
    cotangent,
    seg_ids,
    carry_flags,
    inner_weight,
    inner_velocity,
    inner_average,
    groups_weight,
    groups_velocity,
    groups_average,
    stepper_weight,
    stepper_velocity,
    stepper_average,
    outer_weight,
    outer_velocity,
    outer_average,
    filters_weight,
    filters_velocity,
    filters_average,
    probes_weight,
    probes_velocity,
    probes_average,
    prenorm_weight,
    prenorm_velocity,
    prenorm_average,
    postnorm_weight,
    postnorm_velocity,
    postnorm_average,
    heads_weight,
    heads_velocity,
    heads_average,
):
    local_rows = tokens.shape[0]
    share = tokens.shape[1]
    value_width = filters_weight.shape[1]
    group_width = probes_weight.shape[1]
    heads_local = heads_weight.shape[1]
    span_count = local_rows // CH
    edge_count = KC - 1
    conv_width = value_width + group_width
    pad_heads = group_width - heads_local
    upper = lax.axis_index(HEAD) == 1
    seq_count = lax.axis_size(SEQ)

    shard_a = jnp.concatenate(
        [
            inner_weight[:, 1],
            groups_weight,
            jnp.pad(stepper_weight, ((0, 0), (0, pad_heads))),
        ],
        1,
    ).astype(bf16)
    cut = shard_a.shape[1] // 2
    orders = bit_orders(SEQ)
    far = orders[0][:1:-1]
    near = [order[1::-1] for order in orders]
    begun = gather_rows(shard_a, SEQ, far[:1])
    other = swap(begun, SEQ, 1 << far[1]) if len(far) > 1 else begun
    edge_own = shifted(tokens[local_rows - 8 :], SEQ, 1)
    tokens_ext = jnp.concatenate([edge_own, tokens], 0)
    rows_ext = side_by_side(tokens_ext, swap(tokens_ext, HEAD, 1), upper)
    rows_in = rows_ext[8:]
    rows_ext = rows_ext.astype(f32)
    normed_ext = (
        rows_ext
        * lax.rsqrt(jnp.mean(rows_ext * rows_ext, -1, keepdims=True) + epsilon)
        * prenorm_weight
    ).astype(bf16)
    held_bc = jnp.concatenate(
        [inner_weight[:, 0].astype(bf16), outer_weight.astype(bf16).T], 1
    )
    other, held_bc, normed_ext = lax.optimization_barrier((other, held_bc, normed_ext))
    if len(far) > 1:
        begun = assemble(begun, other, SEQ, far[1], far[:1])
        begun = gather_rows(begun, SEQ, far[2:], far[:2])
    held_a = [begun[:, :cut], begun[:, cut:]]
    other_a = [swap(held_a[k], SEQ, 1 << near[k][0]) for k in range(2)]
    held_bc = after(held_bc, begun)
    other_bc = swap(held_bc, SEQ, 1 << far[0])
    grads_in = side_by_side(cotangent, swap(cotangent, HEAD, 1), upper)
    held_a = [assemble(held_a[k], other_a[k], SEQ, near[k][0], far) for k in range(2)]
    other_a = [swap(held_a[k], SEQ, 1 << near[k][1]) for k in range(2)]
    normed_ext = after(normed_ext, held_a)
    ext_sides = [
        [pick_columns(normed_ext, SEQ, order[0], other) for other in (False, True)]
        for order in orders
    ]
    normed_sides = [[side[8:] for side in sides] for sides in ext_sides]
    held_bc = assemble(held_bc, after(other_bc, held_a), SEQ, far[0], ())
    if len(far) > 1:
        other_bc = swap(held_bc, SEQ, 1 << far[1])
    grads_sides = [pick_columns(grads_in, SEQ, orders[1][0], other) for other in (False, True)]
    own_a = [
        jnp.dot(ext_sides[k][0], held_a[k], preferred_element_type=f32) for k in range(2)
    ]
    other_a, own_a, grads_sides = lax.optimization_barrier((other_a, own_a, grads_sides))
    raw_a = jnp.concatenate(
        lax.optimization_barrier(
            [
                own_a[k] + jnp.dot(ext_sides[k][1], other_a[k], preferred_element_type=f32)
                for k in range(2)
            ]
        ),
        1,
    )
    rows_float = rows_in.astype(f32)
    inverse = lax.rsqrt(jnp.mean(rows_float * rows_float, -1, keepdims=True) + epsilon)
    unit_rows = rows_float * inverse
    normed = (unit_rows * prenorm_weight).astype(bf16)

    other_bc, held_bc, raw_a = lax.optimization_barrier((other_bc, held_bc, raw_a))
    if len(far) > 1:
        held_bc = assemble(held_bc, other_bc, SEQ, far[1], far[:1])
        held_bc = gather_rows(held_bc, SEQ, far[2:], far[:2])
    held_bc = [held_bc[:, :value_width], held_bc[:, value_width:]]
    other_bc = [swap(held_bc[k], SEQ, 1 << near[k][0]) for k in range(2)]
    raw_a = after(raw_a, held_bc)
    step_raw = raw_a[8:, conv_width : conv_width + heads_local]
    extended = lax.reduce_precision(raw_a[8 - edge_count :, :conv_width], 8, 7)
    masks = tap_masks(seg_ids, carry_flags, CH, KC)
    tap_rows = jnp.concatenate([filters_weight, probes_weight], 1)
    conv_out = conv_apply(extended, tap_rows, masks, KC)
    activated = jax.nn.silu(conv_out).astype(bf16)
    own_group = activated[:, value_width:]
    other_group = swap(own_group, HEAD, 1)
    b_rows = jnp.where(upper, other_group, own_group)
    c_rows = jnp.where(upper, own_group, other_group)

    step_pre = step_raw + heads_weight[0]
    step_size = jax.nn.softplus(step_pre)
    decay_rate = -jnp.exp(heads_weight[1])
    log_decay = step_size * decay_rate
    skip_row = expand(heads_weight[2:3])
    seg_spans = seg_ids.reshape(span_count, CH)
    cumulative, entering, leaving, chained = span_edges(
        log_decay.reshape(span_count, CH, heads_local), seg_spans, carry_flags
    )
    cum_t = cumulative.reshape(local_rows, heads_local).T
    step_t = step_size.T
    seg_row = seg_ids.reshape(1, local_rows)
    seg_col = seg_ids.reshape(local_rows, 1)
    enter_wide = expand(entering.reshape(local_rows, heads_local))
    leave_w = leaving.reshape(local_rows, heads_local) * step_size
    leave_wide = expand(leave_w)
    chain_wide = expand(chained)
    factor = jnp.prod(chained, 0)
    b_float = b_rows.astype(f32)
    c_float = c_rows.astype(f32)
    b_spans = b_float.reshape(span_count, CH, N)
    c_spans = c_float.reshape(span_count, CH, N)

    def by_span(array):
        return array.reshape((span_count, CH) + array.shape[1:])

    values_float = activated[:, :value_width].astype(f32)
    local_states = jnp.einsum(
        "cjn,cjw->cnw", b_spans, by_span(values_float * leave_wide), precision=highest
    )
    summary = local_states[0]
    for span in range(1, span_count):
        summary = chain_wide[span] * summary + local_states[span]
    sent_parts = jnp.concatenate(
        [summary, jnp.broadcast_to(jnp.pad(factor, (0, N - heads_local))[None], (N, N))], 1
    )
    pieces = parts_out(sent_parts, SEQ)
    other_bc = after(other_bc, sent_parts)
    held_bc = [assemble(held_bc[k], other_bc[k], SEQ, near[k][0], far) for k in range(2)]
    other_bc = [swap(held_bc[k], SEQ, 1 << near[k][1]) for k in range(2)]
    local_out = span_outputs(
        cum_t, step_t, seg_row, seg_col, b_rows, c_rows, after(activated, held_bc), skip_row
    )
    pieces = after(pieces, local_out)
    factors = expand(pieces[:, 0, value_width : value_width + heads_local])[:, None]
    walked, entered = walked_in(pieces, factors, SEQ, False)
    sides_bc = [normed_sides[0], grads_sides]
    own_bc = [
        jnp.dot(sides_bc[k][0], held_bc[k], preferred_element_type=f32) for k in range(2)
    ]
    entered, own_bc = lax.optimization_barrier((entered, own_bc))
    gate_pre, d_mixed = [
        own_bc[k] + jnp.dot(sides_bc[k][1], other_bc[k], preferred_element_type=f32)
        for k in range(2)
    ]
    enter_rows = entering.reshape(local_rows, heads_local)
    gain_row = postnorm_weight[None]
    carried = (entered, local_states[0], chain_wide[:1])
    middle_args = (local_out, gate_pre, d_mixed, c_rows) + carried + (gain_row, enter_rows)
    row_own = row_sums(*middle_args)
    row_other = swap(row_own, HEAD, 1)
    mixed, d_ssd, d_gate, d_post, pull_total, pull_last = middle(
        *middle_args, row_own, row_other
    )
    d_post = d_post[0]

    def split_features(array):
        lower_half, upper_half = array[:, :share], array[:, share:]
        return (
            jnp.where(upper, upper_half, lower_half),
            jnp.where(upper, lower_half, upper_half),
        )

    def own_features(array):
        own, other = split_features(array)
        return own + swap(other, HEAD, 1)

    def back_product(grads, weights):
        return lax.dot_general(
            grads, weights, (((1,), (1,)), ((), ())), preferred_element_type=f32
        )

    pull_pieces = parts_out(pull_total, SEQ)
    mixed, d_gate = after((mixed, d_gate), pull_total)
    order_c, order_b = orders[1], orders[0]
    half = value_width // 2
    firsts = [1 << order_c[0], 1 << order_b[0]]
    lefts = [grads_sides, normed_sides[0]]
    sent_one = [
        token_product(side[1], grad[:, :half]).astype(bf16)
        for side, grad in zip(lefts, (mixed, d_gate))
    ]
    got_one = [swap(sent, SEQ, mask) for sent, mask in zip(sent_one, firsts)]
    d_ssd = after(d_ssd, sent_one)
    dv_local, d_step_t, d_cum_t, db_local, dc_local = span_backs(
        cum_t, step_t, seg_row, seg_col, b_rows, c_rows, activated, skip_row, d_ssd
    )
    pull_pieces, dv_local = lax.optimization_barrier((pull_pieces, dv_local))
    walked, running = walked_in(pull_pieces, factors, SEQ, True)
    mixed, d_gate = after((mixed, d_gate), walked)
    sent_two = [
        token_product(side[1], grad[:, half:]).astype(bf16)
        for side, grad in zip(lefts, (mixed, d_gate))
    ]
    got_two = [swap(sent, SEQ, mask) for sent, mask in zip(sent_two, firsts)]
    kept_bc = [token_product(side[0], grad) for side, grad in zip(lefts, (mixed, d_gate))]
    running = after(running, kept_bc, sent_two)
    leave_rows = leaving.reshape(local_rows, heads_local)
    d_values, d_b_rows, d_c_rows, d_step, d_log, d_skip = late(
        activated, d_ssd, b_rows, c_rows, *carried, running, pull_last, chain_wide[1:],
        dv_local, db_local, dc_local, d_step_t, d_cum_t, enter_rows, leave_rows, step_size, chained,
    )
    d_skip = jnp.sum(d_skip[:, 0, :heads_local], 0)
    d_step_all = d_step + d_log * decay_rate
    d_alog = jnp.sum(d_log * step_size, 0) * decay_rate
    d_pre = d_step_all * jax.nn.sigmoid(step_pre)
    d_bias = jnp.sum(d_pre, 0)
    d_step_low = d_pre.astype(bf16)

    group_share = jnp.where(upper, d_c_rows, d_b_rows) + swap(
        jnp.where(upper, d_b_rows, d_c_rows), HEAD, 1
    )
    head_grad = jnp.concatenate([d_values[:8], group_share[:8]], 1) * silu_slope(conv_out[:8])
    head_ext = sum(
        jnp.pad(
            tap_rows[lagged] * masks[lagged - 1][:8, None] * head_grad,
            ((edge_count - lagged, lagged), (0, 0)),
        )
        for lagged in range(1, KC)
    )[:edge_count]
    from_next = shifted(head_ext, SEQ, -1)
    got_one, got_two, kept_bc = after((got_one, got_two, kept_bc), head_ext)
    held_bc_grad = [
        kept + jnp.concatenate([one, two], 1).astype(f32)
        for kept, one, two in zip(kept_bc, got_one, got_two)
    ]
    seconds = [order_c[1:], order_b[1:]]
    kept_bc, sent_bc = zip(
        *[sides_of(h, SEQ, left[0], left) for h, left in zip(held_bc_grad, seconds)]
    )
    got_bc = [swap(sent, SEQ, 1 << left[0]) for sent, left in zip(sent_bc, seconds)]
    d_values, group_share = after((d_values, group_share), sent_bc)
    d_conv = jnp.concatenate([d_values, group_share], 1) * silu_slope(conv_out)
    d_taps, ext_grad = conv_backward(extended, tap_rows, masks, d_conv, KC)
    from_next = after(from_next, sent_bc)
    rest = orders[0][2:]
    d_conv_in = ext_grad[edge_count:] + jnp.pad(from_next, ((local_rows - edge_count, 0), (0, 0)))
    grads_a = jnp.concatenate(
        [d_conv_in.astype(bf16), jnp.pad(d_step_low, ((0, 0), (0, pad_heads)))], 1
    )
    parts_a = [grads_a[:, :cut], grads_a[:, cut:]]
    sent_a = [token_product(normed_sides[k][1], parts_a[k]).astype(bf16) for k in range(2)]
    got_a = [swap(sent_a[k], SEQ, 1 << orders[k][0]) for k in range(2)]
    parts_a, held_a, other_a, held_bc, other_bc, got_bc = after(
        (parts_a, held_a, other_a, held_bc, other_bc, got_bc), sent_a
    )
    full_a = [
        assemble(held_a[k], other_a[k], SEQ, near[k][1], far + near[k][:1]) for k in range(2)
    ]
    full_b, full_c = [
        assemble(held_bc[k], other_bc[k], SEQ, near[k][1], far + near[k][:1]) for k in range(2)
    ]
    heads_flat = jnp.concatenate([d_bias, d_alog, d_skip])
    small = jnp.concatenate(
        [
            d_taps,
            jnp.pad(d_post, (0, group_width))[None],
            jnp.pad(heads_flat, (0, conv_width - 3 * heads_local))[None],
        ],
        0,
    )
    small = butterfly_sum(after(small, sent_a), SEQ, orders[0][2:])
    d_normed_own, d_normed_other = split_features(
        back_product(d_gate, full_b)
        + back_product(parts_a[0], full_a[0])
        + back_product(parts_a[1], full_a[1])
    )
    d_normed_got = swap(d_normed_other, HEAD, 1)
    held_bc_grad = [k + g.astype(f32) for k, g in zip(kept_bc, got_bc)]
    kept_bc, sent_bc = zip(*[sides_of(h, SEQ, rest[0], rest) for h in held_bc_grad])
    got_bc = [swap(sent, SEQ, 1 << rest[0]) for sent in sent_bc]
    got_bc = after(got_bc, d_normed_other)
    held_bc_grad = [k + g.astype(f32) for k, g in zip(kept_bc, got_bc)]
    if len(rest) > 1:
        kept_bc, sent_bc = zip(*[sides_of(h, SEQ, rest[1], rest[1:]) for h in held_bc_grad])
        got_bc = [swap(sent, SEQ, 1 << rest[1]) for sent in sent_bc]
    kept_a = [token_product(normed_sides[k][0], parts_a[k]) for k in range(2)]
    kept_a, got_a = after((kept_a, got_a), sent_bc, d_normed_other)
    kept_a, sent_a = zip(
        *[
            sides_of(kept_a[k] + got_a[k].astype(f32), SEQ, orders[k][1], orders[k][1:])
            for k in range(2)
        ]
    )
    got_a = [swap(sent_a[k], SEQ, 1 << orders[k][1]) for k in range(2)]
    d_normed_own, d_normed_got, mixed, full_c = after(
        (d_normed_own, d_normed_got, mixed, full_c), sent_a
    )
    d_normed = d_normed_own + d_normed_got
    own_unit = jnp.where(upper, unit_rows[:, share:], unit_rows[:, :share])
    own_gain = jnp.where(upper, prenorm_weight[share:], prenorm_weight[:share])
    own_rows = tokens.astype(f32)
    d_prenorm = jnp.sum(d_normed * own_unit, 0)
    d_unit_in = d_normed * own_gain
    mean_own = jnp.sum(d_unit_in * own_rows, -1)
    row_mean = ((mean_own + swap(mean_own, HEAD, 1)) / D)[:, None]
    input_gradient = (
        cotangent.astype(f32) + inverse * d_unit_in - own_rows * inverse**3 * row_mean
    )

    held_a = jnp.concatenate([k + g.astype(f32) for k, g in zip(kept_a, got_a)], 1)
    kept_a, sent_a = sides_of(held_a, SEQ, rest[0], rest)
    got_a = swap(sent_a, SEQ, 1 << rest[0])
    small, d_prenorm = after((small, d_prenorm[None]), sent_a)
    small = butterfly_sum(small, SEQ, orders[0][:2])
    d_prenorm = butterfly_sum(d_prenorm, SEQ, orders[0][:2])
    projected = own_features(back_product(mixed, full_c))
    output = (tokens.astype(f32) + projected).astype(bf16)
    held_a = kept_a + got_a.astype(f32)
    kept_a, sent_a = sides_of(held_a, SEQ, rest[1], rest[1:])
    got_a = swap(sent_a, SEQ, 1 << rest[1])
    prenorm_own = butterfly_sum(after(d_prenorm, sent_a), SEQ, rest)
    got_bc = after(got_bc, sent_a)
    if len(rest) > 1:
        held_bc_grad = [k + g.astype(f32) for k, g in zip(kept_bc, got_bc)]
    outer_grad, gate_grad = [scatter_rows(h, SEQ, rest[2:], rest[2:]) for h in held_bc_grad]
    outer_grad = outer_grad.T
    got_a = after(got_a, output, input_gradient)
    rest_grad = scatter_rows(kept_a + got_a.astype(f32), SEQ, rest[2:], rest[2:])
    filters_grad = small[: KC + 1, :value_width]
    probes_grad = small[: KC + 1, value_width:]
    postnorm_grad = small[KC + 1, :value_width]
    prenorm_grad = side_by_side(prenorm_own, swap(prenorm_own, HEAD, 1), upper)[0]
    heads_grad = small[KC + 2, : 3 * heads_local].reshape(3, heads_local)

    groups_grad = rest_grad[:, value_width:conv_width]
    stepper_grad = rest_grad[:, conv_width : conv_width + heads_local]
    root = math.sqrt(local_rows * seq_count)
    inner_new = update_inner(
        inner_weight, inner_velocity, inner_average, gate_grad, rest_grad, D ** (-0.5) / root
    )
    groups_new = apply_update(
        groups_weight, groups_velocity, groups_average, groups_grad, D ** (-0.5) / root
    )
    stepper_new = apply_update(
        stepper_weight, stepper_velocity, stepper_average, stepper_grad, (4 * D) ** (-0.5) / root
    )
    outer_new = apply_update(
        outer_weight, outer_velocity, outer_average, outer_grad, DI ** (-0.5) / root
    )
    filters_new = apply_update(
        filters_weight, filters_velocity, filters_average, filters_grad, 0.5 / root
    )
    probes_new = apply_update(
        probes_weight, probes_velocity, probes_average, probes_grad, 0.5 / root
    )
    prenorm_new = apply_update(
        prenorm_weight, prenorm_velocity, prenorm_average, prenorm_grad, 0.1 / root
    )
    postnorm_new = apply_update(
        postnorm_weight, postnorm_velocity, postnorm_average, postnorm_grad, 0.1 / root
    )
    heads_new = apply_update(heads_weight, heads_velocity, heads_average, heads_grad, 0.5 / root)
    return (
        output,
        input_gradient,
        inner_new[0],
        inner_new[1],
        inner_new[2],
        inner_new[3],
        groups_new[0],
        groups_new[1],
        groups_new[2],
        groups_new[3],
        stepper_new[0],
        stepper_new[1],
        stepper_new[2],
        stepper_new[3],
        outer_new[0],
        outer_new[1],
        outer_new[2],
        outer_new[3],
        filters_new[0],
        filters_new[1],
        filters_new[2],
        filters_new[3],
        probes_new[0],
        probes_new[1],
        probes_new[2],
        probes_new[3],
        prenorm_new[0],
        prenorm_new[1],
        prenorm_new[2],
        prenorm_new[3],
        postnorm_new[0],
        postnorm_new[1],
        postnorm_new[2],
        postnorm_new[3],
        heads_new[0],
        heads_new[1],
        heads_new[2],
        heads_new[3],
    )


def solution(mesh):
    return jax.shard_map(
        shards,
        mesh=mesh,
        in_specs=(
            P(SEQ, HEAD),
            P(SEQ, HEAD),
            P(SEQ),
            P(SEQ),
            P(SEQ, None, HEAD),
            P(SEQ, None, HEAD),
            P(SEQ, None, HEAD),
            P(SEQ, HEAD),
            P(SEQ, HEAD),
            P(SEQ, HEAD),
            P(SEQ, HEAD),
            P(SEQ, HEAD),
            P(SEQ, HEAD),
            P(HEAD, SEQ),
            P(HEAD, SEQ),
            P(HEAD, SEQ),
            P(None, HEAD),
            P(None, HEAD),
            P(None, HEAD),
            P(None, HEAD),
            P(None, HEAD),
            P(None, HEAD),
            P(),
            P(),
            P(),
            P(HEAD),
            P(HEAD),
            P(HEAD),
            P(None, HEAD),
            P(None, HEAD),
            P(None, HEAD),
        ),
        out_specs=(
            P(SEQ, HEAD),
            P(SEQ, HEAD),
            P(SEQ, None, HEAD),
            P(SEQ, None, HEAD),
            P(SEQ, None, HEAD),
            P(SEQ, None, HEAD),
            P(SEQ, HEAD),
            P(SEQ, HEAD),
            P(SEQ, HEAD),
            P(SEQ, HEAD),
            P(SEQ, HEAD),
            P(SEQ, HEAD),
            P(SEQ, HEAD),
            P(SEQ, HEAD),
            P(HEAD, SEQ),
            P(HEAD, SEQ),
            P(HEAD, SEQ),
            P(HEAD, SEQ),
            P(None, HEAD),
            P(None, HEAD),
            P(None, HEAD),
            P(None, HEAD),
            P(None, HEAD),
            P(None, HEAD),
            P(None, HEAD),
            P(None, HEAD),
            P(),
            P(),
            P(),
            P(),
            P(HEAD),
            P(HEAD),
            P(HEAD),
            P(HEAD),
            P(None, HEAD),
            P(None, HEAD),
            P(None, HEAD),
            P(None, HEAD),
        ),
        check_vma=False,
    )
```

```python
import math

import jax
import jax.numpy as jnp
from jax import lax
from jax.experimental import pallas as pl
from jax.experimental.pallas import tpu as pltpu
from jax.sharding import PartitionSpec as P


D = 1536
DI = 3072
P_SIZE = 64
N = 128
KC = 4
CH = 256
HB = 8
SEQ = "seq"
HEAD = "head"


epsilon = 1e-05
momentum_decay = 0.9
average_decay = 0.9
highest = lax.Precision.HIGHEST
f32 = jnp.float32
bf16 = jnp.bfloat16


def shifted(array, axis, by):
    count = lax.axis_size(axis)
    pairs = [(i, i + by) for i in range(count) if 0 <= i + by < count]
    return lax.ppermute(array, axis, pairs)


def swap(array, axis, mask):
    count = lax.axis_size(axis)
    return lax.ppermute(array, axis, [(i, i ^ mask) for i in range(count)])


def bit_orders(axis):
    bits = lax.axis_size(axis).bit_length() - 1
    first = list(range(bits))
    second = first[:]
    if bits > 1:
        second[0], second[1] = 1, 0
    return first, second


def after(values, *others):
    return lax.optimization_barrier((values, others))[0]


def assemble(own, other, axis, bit, done):
    upper = ((lax.axis_index(axis) >> bit) & 1) == 1
    before = 1 << sum(1 for b in done if b > bit)
    split = (before, own.shape[0] // before, own.shape[1])
    own, other = own.reshape(split), other.reshape(split)
    return jnp.stack([jnp.where(upper, other, own), jnp.where(upper, own, other)], 1).reshape(
        2 * split[0] * split[1], split[2]
    )


def gather_rows(held, axis, bits, done=()):
    done = list(done)
    for bit in bits:
        held = assemble(held, swap(held, axis, 1 << bit), axis, bit, done)
        done.append(bit)
    return held


def sides_of(held, axis, bit, left):
    mine = (lax.axis_index(axis) >> bit) & 1
    before = 1 << sum(1 for b in left if b > bit)
    split = held.reshape(before, 2, held.shape[0] // (2 * before), held.shape[1])
    flat = (held.shape[0] // 2, held.shape[1])
    kept = lax.dynamic_index_in_dim(split, mine, 1, False).reshape(flat)
    return kept, lax.dynamic_index_in_dim(split, 1 - mine, 1, False).astype(bf16).reshape(flat)


def scatter_rows(held, axis, bits, left):
    left = list(left)
    for bit in bits:
        kept, sent = sides_of(held, axis, bit, left)
        held = kept + swap(sent, axis, 1 << bit).astype(f32)
        left.remove(bit)
    return held


def pick_columns(array, axis, bit, other):
    mine = (lax.axis_index(axis) >> bit) & 1
    run = (array.shape[1] // lax.axis_size(axis)) << bit
    split = array.reshape(array.shape[0], array.shape[1] // (2 * run), 2, run)
    return lax.dynamic_index_in_dim(split, 1 - mine if other else mine, 2, False).reshape(
        array.shape[0], array.shape[1] // 2
    )


def token_product(left, right):
    return lax.dot_general(left, right, (((0,), (0,)), ((), ())), preferred_element_type=f32)


def butterfly_sum(array, axis, bits):
    for bit in bits:
        array = array + swap(array, axis, 1 << bit)
    return array


def side_by_side(own, other, upper):
    return jnp.concatenate([jnp.where(upper, other, own), jnp.where(upper, own, other)], 1)


def expand(array):
    count = array.shape[-1]
    spread = (
        jnp.arange(count)[:, None] == (jnp.arange(count * P_SIZE) // P_SIZE)[None, :]
    ).astype(f32)
    return jnp.dot(array, spread, precision=highest)


def silu_slope(values):
    sigmoid = jax.nn.sigmoid(values)
    return sigmoid * (1.0 + values * (1.0 - sigmoid))


def tap_masks(seg_rows, flag_rows, span_len, taps):
    number = seg_rows.shape[0]
    within = jnp.arange(number) % span_len
    first_seg = jnp.repeat(seg_rows[::span_len], span_len)
    continued = (jnp.repeat(flag_rows, span_len) == 1) & (seg_rows == first_seg)
    stacked = []
    for lagged in range(1, taps):
        earlier = jnp.concatenate([jnp.full((lagged,), -1, jnp.int32), seg_rows[:-lagged]])
        stacked.append(jnp.where(within >= lagged, earlier == seg_rows, continued))
    return jnp.stack(stacked).astype(jnp.float32)


def conv_apply(extended, tap_rows, masks, taps):
    number = extended.shape[0] - (taps - 1)
    total = tap_rows[taps] + tap_rows[0] * extended[taps - 1 :]
    for lagged in range(1, taps):
        begin = taps - 1 - lagged
        total = (
            total + tap_rows[lagged] * masks[lagged - 1][:, None] * extended[begin : begin + number]
        )
    return total


def conv_backward(extended, tap_rows, masks, grads, taps):
    number = grads.shape[0]
    tap_grads = [jnp.sum(grads * extended[taps - 1 :], 0)]
    ext_grad = jnp.pad(tap_rows[0] * grads, ((taps - 1, 0), (0, 0)))
    for lagged in range(1, taps):
        masked = masks[lagged - 1][:, None] * grads
        begin = taps - 1 - lagged
        tap_grads.append(jnp.sum(masked * extended[begin : begin + number], 0))
        ext_grad = ext_grad + jnp.pad(tap_rows[lagged] * masked, ((begin, lagged), (0, 0)))
    tap_grads.append(jnp.sum(grads, 0))
    return (jnp.stack(tap_grads), ext_grad)


def span_edges(log_decay, seg_spans, flag_spans):
    length = log_decay.shape[1]
    lower = (jnp.arange(length)[:, None] >= jnp.arange(length)[None, :]).astype(f32)
    cumulative = jnp.einsum("ij,cjh->cih", lower, log_decay, precision=highest)
    carried = flag_spans.astype(jnp.float32)[:, None] * (seg_spans == seg_spans[:, :1]).astype(
        jnp.float32
    )
    keeping = (seg_spans == seg_spans[:, -1:]).astype(jnp.float32)
    entering = carried[:, :, None] * jnp.exp(cumulative)
    leaving = keeping[:, :, None] * jnp.exp(cumulative[:, -1:, :] - cumulative)
    chained = carried[:, -1:] * jnp.exp(cumulative[:, -1, :])
    return (cumulative, entering, leaving, chained)


def apply_update(master, velocity, average, gradient, rate_value):
    moment = momentum_decay * velocity + gradient
    stepped = master - rate_value * (gradient + momentum_decay * moment)
    smoothed = average_decay * average + (1.0 - average_decay) * stepped
    return (gradient, stepped, moment, smoothed)


def walk_kernel(count, reverse, part_ref, factor_ref, out_ref):
    def one(turn, state):
        source = count - 1 - turn if reverse else turn
        out_ref[source] = state
        return factor_ref[source] * state + part_ref[source, :, : state.shape[1]]

    lax.fori_loop(0, count, one, jnp.zeros(out_ref.shape[1:], f32))


def parts_out(part, axis):
    count = lax.axis_size(axis)
    pieces = part.reshape((count, part.shape[0] // count) + part.shape[1:])
    return lax.all_to_all(pieces, axis, 0, 0)


def walked_in(pieces, factors, axis, reverse):
    count = lax.axis_size(axis)
    rows, width = pieces.shape[1], factors.shape[2]
    walked = pl.pallas_call(
        lambda *refs: walk_kernel(count, reverse, *refs),
        out_shape=jax.ShapeDtypeStruct((count, rows, width), f32),
        name="walk",
    )(pieces, factors)
    back = lax.all_to_all(walked, axis, 0, 0)
    return walked, back.reshape(count * rows, width)


def update_kernel(rate_value, gate_ref, rest_ref, w_ref, v_ref, a_ref, g_out, w_out, v_out, a_out):
    for k, grad_ref in ((0, gate_ref), (1, rest_ref)):
        grad = grad_ref[...]
        moment = momentum_decay * v_ref[:, k, :] + grad
        stepped = w_ref[:, k, :] - rate_value * (grad + momentum_decay * moment)
        g_out[:, k, :] = grad
        w_out[:, k, :] = stepped
        v_out[:, k, :] = moment
        a_out[:, k, :] = average_decay * a_ref[:, k, :] + (1.0 - average_decay) * stepped


def update_inner(weight, velocity, average, gate_grad, rest_grad, rate_value):
    rows, two, width = weight.shape
    step = 32 if rows % 32 == 0 else rows
    flat = pl.BlockSpec((step, width), lambda r: (r, 0))
    deep = pl.BlockSpec((step, two, width), lambda r: (r, 0, 0))
    return pl.pallas_call(
        lambda *refs: update_kernel(rate_value, *refs),
        grid=(rows // step,),
        in_specs=[flat, flat, deep, deep, deep],
        out_specs=[deep] * 4,
        out_shape=[jax.ShapeDtypeStruct(weight.shape, f32)] * 4,
        name="update_inner",
    )(gate_grad, rest_grad, weight, velocity, average)


def masked_bias(seg_row, seg_col):
    length = seg_row.shape[1]
    rows = lax.broadcasted_iota(jnp.int32, (length, length), 0)
    cols = lax.broadcasted_iota(jnp.int32, (length, length), 1)
    return jnp.where((rows >= cols) & (seg_col == seg_row), 0.0, -1e30).astype(f32)


def inner_product(one, two):
    return lax.dot_general(one, two, (((1,), (1,)), ((), ())), preferred_element_type=f32)


def halves_of(array):
    high = array.astype(bf16)
    return high, (array - high.astype(f32)).astype(bf16)


def exact_dot(left, right, contract=((1,), (0,))):
    return sum(
        lax.dot_general(left, part, (contract, ((), ())), preferred_element_type=f32)
        for part in halves_of(right)
    )


def pair_columns(columns, pair, low_lanes):
    return jnp.where(
        low_lanes, columns[:, 2 * pair : 2 * pair + 1], columns[:, 2 * pair + 1 : 2 * pair + 2]
    )


def entry_state(first_ref, added_ref, chain_ref, lanes):
    first = first_ref[:, lanes]
    return jnp.where(
        pl.program_id(0) == 0, first, chain_ref[:, lanes] * first + added_ref[:, lanes]
    )


def gated_pieces(refs, pair, low_lanes, enter):
    local_ref, gate_ref, mixed_ref, c_ref, first_ref, added_ref, chain_ref, gain_ref = refs
    lanes = pl.ds(pair * 2 * P_SIZE, 2 * P_SIZE)
    enter_pair = pair_columns(enter, pair, low_lanes)
    states = entry_state(first_ref, added_ref, chain_ref, lanes)
    out = local_ref[:, lanes] + enter_pair * exact_dot(c_ref[...], states)
    gate = gate_ref[:, lanes]
    sigmoid = 1.0 / (1.0 + jnp.exp(-gate))
    act = gate * sigmoid
    return out, gate, sigmoid, act, out * act, mixed_ref[:, lanes], gain_ref[:, lanes], enter_pair


def row_sums_kernel(*refs):
    refs, (enter_ref, out_ref) = refs[:8], refs[8:]
    enter = enter_ref[...]
    lane = lax.broadcasted_iota(jnp.int32, (CH, 2 * P_SIZE), 1)
    squares = jnp.zeros((CH, 2 * P_SIZE), f32)
    dots = jnp.zeros((CH, 2 * P_SIZE), f32)
    for pair in range(refs[0].shape[1] // (2 * P_SIZE)):
        gated, d_mixed, gain = gated_pieces(refs, pair, lane < P_SIZE, enter)[4:7]
        squares = squares + gated * gated
        dots = dots + d_mixed * gain * gated
    out_ref[...] = jnp.where(
        lane == 0,
        jnp.sum(squares, 1, keepdims=True),
        jnp.where(lane == 1, jnp.sum(dots, 1, keepdims=True), 0.0),
    )


def middle_specs(width, heads):
    wide = pl.BlockSpec((CH, width), lambda s: (s, 0))
    state = pl.BlockSpec((N, width), lambda s: (0, 0))
    row = pl.BlockSpec((1, width), lambda s: (0, 0))
    group = pl.BlockSpec((CH, N), lambda s: (s, 0))
    return [wide, wide, wide, group, state, state, row, row, pl.BlockSpec((CH, heads), lambda s: (s, 0))]


def row_sums(*args):
    rows, width = args[0].shape
    return pl.pallas_call(
        row_sums_kernel,
        grid=(rows // CH,),
        in_specs=middle_specs(width, args[-1].shape[1]),
        out_specs=pl.BlockSpec((CH, 2 * P_SIZE), lambda s: (s, 0)),
        out_shape=jax.ShapeDtypeStruct((rows, 2 * P_SIZE), f32),
        name="row_sums",
    )(*args)


def middle_kernel(*all_refs):
    refs, (enter_ref, own_ref, other_ref) = all_refs[:8], all_refs[8:11]
    mixed_out, ssd_out, gate_out, post_out, total_out, last_out = all_refs[11:]
    c_ref, chain_ref = refs[3], refs[6]

    @pl.when(pl.program_id(0) == 0)
    def _():
        post_out[...] = jnp.zeros_like(post_out)
        total_out[...] = jnp.zeros_like(total_out)

    enter = enter_ref[...]
    both = own_ref[...] + other_ref[...]
    scale = lax.rsqrt(both[:, 0:1] / DI + epsilon)
    pulled = scale * scale * scale * (both[:, 1:2] / DI)
    low_lanes = lax.broadcasted_iota(jnp.int32, (CH, 2 * P_SIZE), 1) < P_SIZE
    for pair in range(refs[0].shape[1] // (2 * P_SIZE)):
        lanes = pl.ds(pair * 2 * P_SIZE, 2 * P_SIZE)
        out, gate, sigmoid, act, gated, d_mixed, gain, enter_pair = gated_pieces(
            refs, pair, low_lanes, enter
        )
        mixed_out[:, lanes] = (gated * scale * gain).astype(bf16)
        d_gated = scale * (d_mixed * gain) - gated * pulled
        d_ssd = (d_gated * act).astype(bf16)
        ssd_out[:, lanes] = d_ssd
        gate_out[:, lanes] = (d_gated * out * (sigmoid * (1.0 + gate * (1.0 - sigmoid)))).astype(bf16)
        post_out[:, lanes] += jnp.sum(d_mixed * gated * scale, 0, keepdims=True)
        pull = exact_dot(c_ref[...], enter_pair * d_ssd.astype(f32), ((0,), (0,)))
        total_out[:, lanes] += jnp.where(pl.program_id(0) == 0, 1.0, chain_ref[:, lanes]) * pull
        last_out[:, lanes] = pull


def middle(*args):
    rows, width = args[0].shape
    wide = pl.BlockSpec((CH, width), lambda s: (s, 0))
    state = pl.BlockSpec((N, width), lambda s: (0, 0))
    low = jax.ShapeDtypeStruct((rows, width), bf16)
    return pl.pallas_call(
        middle_kernel,
        grid=(rows // CH,),
        in_specs=middle_specs(width, args[-3].shape[1])
        + [pl.BlockSpec((CH, 2 * P_SIZE), lambda s: (s, 0))] * 2,
        out_specs=[wide, wide, wide, pl.BlockSpec((1, width), lambda s: (0, 0)), state, state],
        out_shape=[
            low,
            low,
            low,
            jax.ShapeDtypeStruct((1, width), f32),
            jax.ShapeDtypeStruct((N, width), f32),
            jax.ShapeDtypeStruct((N, width), f32),
        ],
        name="middle",
    )(*args)


def late_kernel(v_ref, g_ref, b_ref, c_ref, first_ref, added_ref, chain_first_ref, exit_ref, pull_ref,
                chain_last_ref, dv_ref, db_ref, dc_ref, dstep_ref, dcum_ref, enter_ref, leave_ref,
                step_ref, chain_ref, dv_out, db_out, dc_out, dstep_out, dlog_out, dskip_out):
    enter, leave, step = enter_ref[...], leave_ref[...], step_ref[...]
    heads = enter.shape[1]
    wide = 2 * P_SIZE
    lane = lax.broadcasted_iota(jnp.int32, (CH, wide), 1)
    low_lanes = lane < P_SIZE
    from_lane = lax.broadcasted_iota(jnp.int32, (wide, wide), 0)
    to_head = lax.broadcasted_iota(jnp.int32, (wide, wide), 1)
    leave_w = leave * step
    d_leave = jnp.zeros((CH, wide), f32)
    d_enter = jnp.zeros((CH, wide), f32)
    d_chain = jnp.zeros((8, wide), f32)
    d_skip = jnp.zeros((8, wide), f32)
    last_span = pl.program_id(0) == pl.num_programs(0) - 1
    d_b, d_c = db_ref[...], dc_ref[...]
    b_low, c_low = b_ref[...], c_ref[...]

    def summed(array, pick):
        high, rest = halves_of(array)
        return jnp.dot(high, pick, preferred_element_type=f32) + jnp.dot(
            rest, pick, preferred_element_type=f32
        )

    def crossed(one, two):
        one_high, one_rest = halves_of(one)
        two_high, two_rest = halves_of(two)
        return (
            inner_product(one_high, two_high)
            + inner_product(one_high, two_rest)
            + inner_product(one_rest, two_high)
        )

    for pair in range(heads // 2):
        lanes = pl.ds(pair * wide, wide)
        pick = (to_head == 2 * pair + from_lane // P_SIZE).astype(f32).astype(bf16)
        values = v_ref[:, lanes].astype(f32)
        grads = g_ref[:, lanes].astype(f32)
        states = entry_state(first_ref, added_ref, chain_first_ref, lanes)
        nexts = exit_ref[:, lanes]
        nexts = jnp.where(last_span, nexts, chain_last_ref[:, lanes] * nexts + pull_ref[:, lanes])
        leave_pair = pair_columns(leave_w, pair, low_lanes)
        b_pull = exact_dot(b_low, nexts)
        dv_out[:, lanes] = dv_ref[:, lanes] + leave_pair * b_pull
        d_leave = d_leave + summed(values * b_pull, pick)
        d_b = d_b + crossed(values * leave_pair, nexts)
        d_enter = d_enter + summed(grads * exact_dot(c_low, states), pick)
        d_c = d_c + crossed(pair_columns(enter, pair, low_lanes) * grads, states)
        column = jnp.sum(nexts * states, 0, keepdims=True)
        d_chain = d_chain + summed(jnp.broadcast_to(column, (8, wide)), pick)
        column = jnp.sum(grads * values, 0, keepdims=True)
        d_skip = d_skip + summed(jnp.broadcast_to(column, (8, wide)), pick)
    dskip_out[0] = d_skip
    db_out[...] = d_b
    dc_out[...] = d_c
    d_leave, d_enter, d_chain = d_leave[:, :heads], d_enter[:, :heads], d_chain[:1, :heads]
    dstep_out[...] = dstep_ref[...].T + d_leave * leave
    pulled = d_leave * leave_w
    d_cum = dcum_ref[...].T - pulled + d_enter * enter
    at_or_after = (
        lax.broadcasted_iota(jnp.int32, (CH, CH), 0) <= lax.broadcasted_iota(jnp.int32, (CH, CH), 1)
    ).astype(f32)
    last = jnp.sum(pulled, 0, keepdims=True) + d_chain * chain_ref[0]
    dlog_out[...] = jnp.dot(at_or_after, d_cum, precision=highest) + last


def late(values, grads, b_rows, c_rows, first, added, chain_first, last, pull, chain_last, dv, db, dc,
         d_step_t, d_cum_t, enter, leave, step, chained):
    rows, width = grads.shape
    heads = width // P_SIZE
    wide = pl.BlockSpec((CH, width), lambda s: (s, 0))
    group = pl.BlockSpec((CH, N), lambda s: (s, 0))
    state = pl.BlockSpec((N, width), lambda s: (0, 0))
    row = pl.BlockSpec((1, width), lambda s: (0, 0))
    turned = pl.BlockSpec((heads, CH), lambda s: (0, s))
    thin = pl.BlockSpec((CH, heads), lambda s: (s, 0))
    one = pl.BlockSpec((1, 1, heads), lambda s: (s, 0, 0))
    return pl.pallas_call(
        late_kernel,
        grid=(rows // CH,),
        in_specs=[wide, wide, group, group, state, state, row, state, state, row, wide, group, group,
                  turned, turned, thin, thin, thin, one],
        out_specs=[wide, group, group, thin, thin,
                   pl.BlockSpec((1, 8, 2 * P_SIZE), lambda s: (s, 0, 0))],
        out_shape=[
            jax.ShapeDtypeStruct((rows, width), f32),
            jax.ShapeDtypeStruct((rows, N), f32),
            jax.ShapeDtypeStruct((rows, N), f32),
            jax.ShapeDtypeStruct((rows, heads), f32),
            jax.ShapeDtypeStruct((rows, heads), f32),
            jax.ShapeDtypeStruct((rows // CH, 8, 2 * P_SIZE), f32),
        ],
        name="late",
    )(values, grads, b_rows, c_rows, first, added, chain_first, last, pull, chain_last, dv, db, dc,
      d_step_t, d_cum_t, enter, leave, step, chained[:, None])


def span_kernel(cum_ref, step_ref, seg_row_ref, seg_col_ref, b_ref, c_ref, v_ref, skip_ref, y_ref,
                scores_ref, bias_ref):
    @pl.when(pl.program_id(1) == 0)
    def _():
        scores_ref[...] = inner_product(c_ref[...], b_ref[...])
        bias_ref[...] = masked_bias(seg_row_ref[...], seg_col_ref[...])

    cum_rows = cum_ref[...]
    cum_cols = cum_rows.T
    step_rows = step_ref[...]
    low_lanes = lax.broadcasted_iota(jnp.int32, (CH, 2 * P_SIZE), 1) < P_SIZE
    for pair in range(HB // 2):
        lanes = pl.ds(pair * 2 * P_SIZE, 2 * P_SIZE)
        v_pair = v_ref[:, lanes]
        both = []
        for h in (2 * pair, 2 * pair + 1):
            decay = jnp.exp(cum_cols[:, h : h + 1] - cum_rows[h : h + 1, :] + bias_ref[...])
            mixing = (scores_ref[...] * decay * step_rows[h : h + 1, :]).astype(bf16)
            both.append(jnp.dot(mixing, v_pair, preferred_element_type=f32))
        y_ref[:, lanes] = (
            jnp.where(low_lanes, both[0], both[1]) + skip_ref[:, lanes] * v_pair.astype(f32)
        )


def span_outputs(cum_t, step_t, seg_row, seg_col, b_rows, c_rows, values, skip_row):
    rows, width = values.shape[0], skip_row.shape[1]
    wide = HB * P_SIZE
    return pl.pallas_call(
        span_kernel,
        grid=(rows // CH, width // wide),
        in_specs=[
            pl.BlockSpec((HB, CH), lambda s, g: (g, s)),
            pl.BlockSpec((HB, CH), lambda s, g: (g, s)),
            pl.BlockSpec((1, CH), lambda s, g: (0, s)),
            pl.BlockSpec((CH, 1), lambda s, g: (s, 0)),
            pl.BlockSpec((CH, N), lambda s, g: (s, 0)),
            pl.BlockSpec((CH, N), lambda s, g: (s, 0)),
            pl.BlockSpec((CH, wide), lambda s, g: (s, g)),
            pl.BlockSpec((1, wide), lambda s, g: (0, g)),
        ],
        out_specs=pl.BlockSpec((CH, wide), lambda s, g: (s, g)),
        out_shape=jax.ShapeDtypeStruct((rows, width), f32),
        scratch_shapes=[pltpu.VMEM((CH, CH), f32), pltpu.VMEM((CH, CH), f32)],
        name="span_outputs",
    )(cum_t, step_t, seg_row, seg_col, b_rows, c_rows, values, skip_row)


def span_back_kernel(cum_ref, step_ref, seg_row_ref, seg_col_ref, b_ref, c_ref, v_ref, skip_ref, g_ref,
                     dv_ref, dstep_ref, dcum_ref, db_ref, dc_ref, scores_ref, bias_ref, total_ref):
    @pl.when(pl.program_id(1) == 0)
    def _():
        scores_ref[...] = inner_product(c_ref[...], b_ref[...])
        bias_ref[...] = masked_bias(seg_row_ref[...], seg_col_ref[...])
        total_ref[...] = jnp.zeros_like(total_ref)

    cum_rows = cum_ref[...]
    cum_cols = cum_rows.T
    step_rows = step_ref[...]
    lane = lax.broadcasted_iota(jnp.int32, (CH, 2 * P_SIZE), 1)
    low_lanes = lane < P_SIZE
    row_sums = jnp.zeros((CH, 2 * P_SIZE), f32)
    zero = jnp.zeros((), bf16)
    for pair in range(HB // 2):
        lanes = pl.ds(pair * 2 * P_SIZE, 2 * P_SIZE)
        v_pair = v_ref[:, lanes]
        g_pair = g_ref[:, lanes]
        both = []
        for h in (2 * pair, 2 * pair + 1):
            step_row = step_rows[h : h + 1, :]
            scores = scores_ref[...]
            decay = jnp.exp(cum_cols[:, h : h + 1] - cum_rows[h : h + 1, :] + bias_ref[...])
            mixing_f = decay * step_row
            mixing = (scores * decay * step_row).astype(bf16)
            own = low_lanes if h % 2 == 0 else jnp.logical_not(low_lanes)
            d_mix = inner_product(jnp.where(own, g_pair, zero), v_pair)
            both.append(
                lax.dot_general(mixing, g_pair, (((0,), (0,)), ((), ())), preferred_element_type=f32)
            )
            total_ref[...] += d_mix * mixing_f
            weighted = d_mix * scores * decay
            column = jnp.sum(weighted, 0, keepdims=True)
            dstep_ref[h : h + 1, :] = column
            dcum_ref[h : h + 1, :] = -column * step_row
            row_sums = row_sums + jnp.where(
                lane == h, jnp.sum(weighted * step_row, 1, keepdims=True), 0.0
            )
        dv_ref[:, lanes] = (
            jnp.where(low_lanes, both[0], both[1]) + skip_ref[:, lanes] * g_pair.astype(f32)
        )
    dcum_ref[...] += row_sums.T[:HB, :]

    @pl.when(pl.program_id(1) == pl.num_programs(1) - 1)
    def _():
        total = total_ref[...]
        dc_ref[...] = jnp.dot(total, b_ref[...].astype(f32), precision=highest)
        db_ref[...] = jnp.dot(total.T, c_ref[...].astype(f32), precision=highest)


def span_backs(cum_t, step_t, seg_row, seg_col, b_rows, c_rows, values, skip_row, grads):
    rows, width = grads.shape
    wide = HB * P_SIZE
    heads = width // P_SIZE
    return pl.pallas_call(
        span_back_kernel,
        grid=(rows // CH, width // wide),
        in_specs=[
            pl.BlockSpec((HB, CH), lambda s, g: (g, s)),
            pl.BlockSpec((HB, CH), lambda s, g: (g, s)),
            pl.BlockSpec((1, CH), lambda s, g: (0, s)),
            pl.BlockSpec((CH, 1), lambda s, g: (s, 0)),
            pl.BlockSpec((CH, N), lambda s, g: (s, 0)),
            pl.BlockSpec((CH, N), lambda s, g: (s, 0)),
            pl.BlockSpec((CH, wide), lambda s, g: (s, g)),
            pl.BlockSpec((1, wide), lambda s, g: (0, g)),
            pl.BlockSpec((CH, wide), lambda s, g: (s, g)),
        ],
        out_specs=[
            pl.BlockSpec((CH, wide), lambda s, g: (s, g)),
            pl.BlockSpec((HB, CH), lambda s, g: (g, s)),
            pl.BlockSpec((HB, CH), lambda s, g: (g, s)),
            pl.BlockSpec((CH, N), lambda s, g: (s, 0)),
            pl.BlockSpec((CH, N), lambda s, g: (s, 0)),
        ],
        out_shape=[
            jax.ShapeDtypeStruct((rows, width), f32),
            jax.ShapeDtypeStruct((heads, rows), f32),
            jax.ShapeDtypeStruct((heads, rows), f32),
            jax.ShapeDtypeStruct((rows, N), f32),
            jax.ShapeDtypeStruct((rows, N), f32),
        ],
        scratch_shapes=[pltpu.VMEM((CH, CH), f32)] * 3,
        name="span_backs",
    )(cum_t, step_t, seg_row, seg_col, b_rows, c_rows, values, skip_row, grads)


def shards(
    tokens,
    cotangent,
    seg_ids,
    carry_flags,
    inner_weight,
    inner_velocity,
    inner_average,
    groups_weight,
    groups_velocity,
    groups_average,
    stepper_weight,
    stepper_velocity,
    stepper_average,
    outer_weight,
    outer_velocity,
    outer_average,
    filters_weight,
    filters_velocity,
    filters_average,
    probes_weight,
    probes_velocity,
    probes_average,
    prenorm_weight,
    prenorm_velocity,
    prenorm_average,
    postnorm_weight,
    postnorm_velocity,
    postnorm_average,
    heads_weight,
    heads_velocity,
    heads_average,
):
    local_rows = tokens.shape[0]
    share = tokens.shape[1]
    value_width = filters_weight.shape[1]
    group_width = probes_weight.shape[1]
    heads_local = heads_weight.shape[1]
    span_count = local_rows // CH
    edge_count = KC - 1
    conv_width = value_width + group_width
    pad_heads = group_width - heads_local
    upper = lax.axis_index(HEAD) == 1
    seq_count = lax.axis_size(SEQ)

    shard_a = jnp.concatenate(
        [
            inner_weight[:, 1],
            groups_weight,
            jnp.pad(stepper_weight, ((0, 0), (0, pad_heads))),
        ],
        1,
    ).astype(bf16)
    cut = shard_a.shape[1] // 2
    orders = bit_orders(SEQ)
    far = orders[0][:1:-1]
    near = [order[1::-1] for order in orders]
    begun = gather_rows(shard_a, SEQ, far[:1], ())
    other = swap(begun, SEQ, 1 << far[1]) if len(far) > 1 else begun
    edge_own = shifted(tokens[local_rows - 8 :], SEQ, 1)
    tokens_ext = jnp.concatenate([edge_own, tokens], 0)
    rows_ext = side_by_side(tokens_ext, swap(tokens_ext, HEAD, 1), upper)
    rows_in = rows_ext[8:]
    rows_ext = rows_ext.astype(f32)
    normed_ext = (
        rows_ext
        * lax.rsqrt(jnp.mean(rows_ext * rows_ext, -1, keepdims=True) + epsilon)
        * prenorm_weight
    ).astype(bf16)
    held_bc = jnp.concatenate(
        [inner_weight[:, 0].astype(bf16), outer_weight.astype(bf16).T], 1
    )
    other, held_bc, normed_ext = lax.optimization_barrier((other, held_bc, normed_ext))
    if len(far) > 1:
        begun = assemble(begun, other, SEQ, far[1], far[:1])
        begun = gather_rows(begun, SEQ, far[2:], far[:2])
    held_a = [begun[:, :cut], begun[:, cut:]]
    other_a = [swap(held_a[k], SEQ, 1 << near[k][0]) for k in range(2)]
    held_bc = after(held_bc, begun)
    other_bc = swap(held_bc, SEQ, 1 << far[0])
    grads_got = swap(cotangent, HEAD, 1)
    held_a = [assemble(held_a[k], other_a[k], SEQ, near[k][0], far) for k in range(2)]
    other_a = [swap(held_a[k], SEQ, 1 << near[k][1]) for k in range(2)]
    normed_ext, grads_got = after((normed_ext, grads_got), held_a)
    grads_in = side_by_side(cotangent, grads_got, upper)
    ext_sides = [
        [pick_columns(normed_ext, SEQ, order[0], other) for other in (False, True)]
        for order in orders
    ]
    normed_sides = [[side[8:] for side in sides] for sides in ext_sides]
    held_bc = assemble(held_bc, after(other_bc, held_a), SEQ, far[0], ())
    if len(far) > 1:
        other_bc = swap(held_bc, SEQ, 1 << far[1])
    grads_sides = [pick_columns(grads_in, SEQ, orders[1][0], other) for other in (False, True)]
    own_a = [
        jnp.dot(ext_sides[k][0], held_a[k], preferred_element_type=f32) for k in range(2)
    ]
    other_a, own_a, grads_sides = lax.optimization_barrier((other_a, own_a, grads_sides))
    raw_a = jnp.concatenate(
        lax.optimization_barrier(
            [
                own_a[k] + jnp.dot(ext_sides[k][1], other_a[k], preferred_element_type=f32)
                for k in range(2)
            ]
        ),
        1,
    )
    rows_float = rows_in.astype(f32)
    inverse = lax.rsqrt(jnp.mean(rows_float * rows_float, -1, keepdims=True) + epsilon)
    unit_rows = rows_float * inverse
    normed = (unit_rows * prenorm_weight).astype(bf16)

    other_bc, held_bc, raw_a = lax.optimization_barrier((other_bc, held_bc, raw_a))
    if len(far) > 1:
        held_bc = assemble(held_bc, other_bc, SEQ, far[1], far[:1])
        held_bc = gather_rows(held_bc, SEQ, far[2:], far[:2])
    held_bc = [held_bc[:, :value_width], held_bc[:, value_width:]]
    other_bc = [swap(held_bc[k], SEQ, 1 << near[k][0]) for k in range(2)]
    raw_a = after(raw_a, held_bc)
    step_raw = raw_a[8:, conv_width : conv_width + heads_local]
    extended = lax.reduce_precision(raw_a[8 - edge_count :, :conv_width], 8, 7)
    masks = tap_masks(seg_ids, carry_flags, CH, KC)
    tap_rows = jnp.concatenate([filters_weight, probes_weight], 1)
    conv_out = conv_apply(extended, tap_rows, masks, KC)
    activated = jax.nn.silu(conv_out).astype(bf16)
    own_group = activated[:, value_width:]
    other_group = swap(own_group, HEAD, 1)
    b_rows = jnp.where(upper, other_group, own_group)
    c_rows = jnp.where(upper, own_group, other_group)

    step_pre = step_raw + heads_weight[0]
    step_size = jax.nn.softplus(step_pre)
    decay_rate = -jnp.exp(heads_weight[1])
    log_decay = step_size * decay_rate
    skip_row = expand(heads_weight[2:3])
    seg_spans = seg_ids.reshape(span_count, CH)
    cumulative, entering, leaving, chained = span_edges(
        log_decay.reshape(span_count, CH, heads_local), seg_spans, carry_flags
    )
    cum_t = cumulative.reshape(local_rows, heads_local).T
    step_t = step_size.T
    seg_row = seg_ids.reshape(1, local_rows)
    seg_col = seg_ids.reshape(local_rows, 1)
    enter_wide = expand(entering.reshape(local_rows, heads_local))
    leave_w = leaving.reshape(local_rows, heads_local) * step_size
    leave_wide = expand(leave_w)
    chain_wide = expand(chained)
    factor = jnp.prod(chained, 0)
    b_float = b_rows.astype(f32)
    c_float = c_rows.astype(f32)
    b_spans = b_float.reshape(span_count, CH, N)
    c_spans = c_float.reshape(span_count, CH, N)

    def by_span(array):
        return array.reshape((span_count, CH) + array.shape[1:])

    values_float = activated[:, :value_width].astype(f32)
    local_states = jnp.einsum(
        "cjn,cjw->cnw", b_spans, by_span(values_float * leave_wide), precision=highest
    )
    summary = local_states[0]
    for span in range(1, span_count):
        summary = chain_wide[span] * summary + local_states[span]
    sent_parts = jnp.concatenate(
        [summary, jnp.broadcast_to(jnp.pad(factor, (0, N - heads_local))[None], (N, N))], 1
    )
    pieces = parts_out(sent_parts, SEQ)
    other_bc = after(other_bc, sent_parts)
    held_bc = [assemble(held_bc[k], other_bc[k], SEQ, near[k][0], far) for k in range(2)]
    other_bc = [swap(held_bc[k], SEQ, 1 << near[k][1]) for k in range(2)]
    local_out = span_outputs(
        cum_t, step_t, seg_row, seg_col, b_rows, c_rows, after(activated, held_bc), skip_row
    )
    pieces = after(pieces, local_out)
    factors = expand(pieces[:, 0, value_width : value_width + heads_local])[:, None]
    walked, entered = walked_in(pieces, factors, SEQ, False)
    sides_bc = [normed_sides[0], grads_sides]
    own_bc = [
        jnp.dot(sides_bc[k][0], held_bc[k], preferred_element_type=f32) for k in range(2)
    ]
    entered, own_bc = lax.optimization_barrier((entered, own_bc))
    gate_pre, d_mixed = [
        own_bc[k] + jnp.dot(sides_bc[k][1], other_bc[k], preferred_element_type=f32)
        for k in range(2)
    ]
    enter_rows = entering.reshape(local_rows, heads_local)
    gain_row = postnorm_weight[None]
    carried = (entered, local_states[0], chain_wide[:1])
    middle_args = (local_out, gate_pre, d_mixed, c_rows) + carried + (gain_row, enter_rows)
    row_own = row_sums(*middle_args)
    row_other = swap(row_own, HEAD, 1)
    mixed, d_ssd, d_gate, d_post, pull_total, pull_last = middle(
        *middle_args, row_own, row_other
    )
    d_post = d_post[0]

    def split_features(array):
        lower_half, upper_half = array[:, :share], array[:, share:]
        return (
            jnp.where(upper, upper_half, lower_half),
            jnp.where(upper, lower_half, upper_half),
        )

    def own_features(array):
        own, other = split_features(array)
        return own + swap(other, HEAD, 1)

    def back_product(grads, weights):
        return lax.dot_general(
            grads, weights, (((1,), (1,)), ((), ())), preferred_element_type=f32
        )

    pull_pieces = parts_out(pull_total, SEQ)
    mixed, d_gate = after((mixed, d_gate), pull_total)
    order_c, order_b = orders[1], orders[0]
    half = value_width // 2
    firsts = [1 << order_c[0], 1 << order_b[0]]
    lefts = [grads_sides, normed_sides[0]]
    sent_one = [
        token_product(side[1], grad[:, :half]).astype(bf16)
        for side, grad in zip(lefts, (mixed, d_gate))
    ]
    got_one = [swap(sent, SEQ, mask) for sent, mask in zip(sent_one, firsts)]
    d_ssd = after(d_ssd, sent_one)
    dv_local, d_step_t, d_cum_t, db_local, dc_local = span_backs(
        cum_t, step_t, seg_row, seg_col, b_rows, c_rows, activated, skip_row, d_ssd
    )
    pull_pieces, dv_local = lax.optimization_barrier((pull_pieces, dv_local))
    walked, running = walked_in(pull_pieces, factors, SEQ, True)
    mixed, d_gate = after((mixed, d_gate), walked)
    sent_two = [
        token_product(side[1], grad[:, half:]).astype(bf16)
        for side, grad in zip(lefts, (mixed, d_gate))
    ]
    got_two = [swap(sent, SEQ, mask) for sent, mask in zip(sent_two, firsts)]
    kept_bc = [token_product(side[0], grad) for side, grad in zip(lefts, (mixed, d_gate))]
    running = after(running, kept_bc, sent_two)
    leave_rows = leaving.reshape(local_rows, heads_local)
    d_values, d_b_rows, d_c_rows, d_step, d_log, d_skip = late(
        activated, d_ssd, b_rows, c_rows, *carried, running, pull_last, chain_wide[1:],
        dv_local, db_local, dc_local, d_step_t, d_cum_t, enter_rows, leave_rows, step_size, chained,
    )
    d_skip = jnp.sum(d_skip[:, 0, :heads_local], 0)
    d_step_all = d_step + d_log * decay_rate
    d_alog = jnp.sum(d_log * step_size, 0) * decay_rate
    d_pre = d_step_all * jax.nn.sigmoid(step_pre)
    d_bias = jnp.sum(d_pre, 0)
    d_step_low = d_pre.astype(bf16)

    group_share = jnp.where(upper, d_c_rows, d_b_rows) + swap(
        jnp.where(upper, d_b_rows, d_c_rows), HEAD, 1
    )
    head_grad = jnp.concatenate([d_values[:8], group_share[:8]], 1) * silu_slope(conv_out[:8])
    head_ext = sum(
        jnp.pad(
            tap_rows[lagged] * masks[lagged - 1][:8, None] * head_grad,
            ((edge_count - lagged, lagged), (0, 0)),
        )
        for lagged in range(1, KC)
    )[:edge_count]
    from_next = shifted(head_ext, SEQ, -1)
    got_one, got_two, kept_bc = after((got_one, got_two, kept_bc), head_ext)
    held_bc_grad = [
        kept + jnp.concatenate([one, two], 1).astype(f32)
        for kept, one, two in zip(kept_bc, got_one, got_two)
    ]
    seconds = [order_c[1:], order_b[1:]]
    kept_bc, sent_bc = zip(
        *[sides_of(h, SEQ, left[0], left) for h, left in zip(held_bc_grad, seconds)]
    )
    got_bc = [swap(sent, SEQ, 1 << left[0]) for sent, left in zip(sent_bc, seconds)]
    d_values, group_share = after((d_values, group_share), sent_bc)
    d_conv = jnp.concatenate([d_values, group_share], 1) * silu_slope(conv_out)
    d_taps, ext_grad = conv_backward(extended, tap_rows, masks, d_conv, KC)
    from_next = after(from_next, sent_bc)
    d_conv_in = ext_grad[edge_count:] + jnp.pad(from_next, ((local_rows - edge_count, 0), (0, 0)))
    grads_a = jnp.concatenate(
        [d_conv_in.astype(bf16), jnp.pad(d_step_low, ((0, 0), (0, pad_heads)))], 1
    )
    rest = orders[0][2:]
    heads_flat = jnp.concatenate([d_bias, d_alog, d_skip])
    small = jnp.concatenate(
        [
            d_taps,
            jnp.pad(d_post, (0, group_width))[None],
            jnp.pad(heads_flat, (0, conv_width - 3 * heads_local))[None],
        ],
        0,
    )
    small = butterfly_sum(small, SEQ, rest)
    parts_a = [grads_a[:, :cut], grads_a[:, cut:]]
    sent_a = [token_product(normed_sides[k][1], parts_a[k]).astype(bf16) for k in range(2)]
    got_a = [swap(sent_a[k], SEQ, 1 << orders[k][0]) for k in range(2)]
    parts_a, held_a, other_a, held_bc, other_bc = after(
        (parts_a, held_a, other_a, held_bc, other_bc), sent_a
    )
    kept_bc, got_bc = after((kept_bc, got_bc), sent_a)
    held_bc_grad = [k + g.astype(f32) for k, g in zip(kept_bc, got_bc)]
    kept_bc, sent_bc = zip(*[sides_of(h, SEQ, rest[0], rest) for h in held_bc_grad])
    got_bc = [swap(sent, SEQ, 1 << rest[0]) for sent in sent_bc]
    held_a = after(held_a, sent_bc)
    full_a = [
        assemble(held_a[k], other_a[k], SEQ, near[k][1], far + near[k][:1]) for k in range(2)
    ]
    full_b = assemble(held_bc[0], other_bc[0], SEQ, near[0][1], far + near[0][:1])
    d_normed_part = (
        back_product(d_gate, full_b)
        + back_product(parts_a[0], full_a[0])
        + back_product(parts_a[1], full_a[1])
    )
    got_bc = after(got_bc, d_normed_part)
    held_bc_grad = [k + g.astype(f32) for k, g in zip(kept_bc, got_bc)]
    if len(rest) > 1:
        kept_bc, sent_bc = zip(*[sides_of(h, SEQ, rest[1], rest[1:]) for h in held_bc_grad])
        got_bc = [swap(sent, SEQ, 1 << rest[1]) for sent in sent_bc]
    d_normed_own, d_normed_other = split_features(d_normed_part)
    d_normed_got = swap(d_normed_other, HEAD, 1)
    kept_a = [token_product(normed_sides[k][0], parts_a[k]) for k in range(2)]
    kept_a, got_a = after((kept_a, got_a), d_normed_other, sent_bc)
    kept_a, sent_a = zip(
        *[
            sides_of(kept_a[k] + got_a[k].astype(f32), SEQ, orders[k][1], orders[k][1:])
            for k in range(2)
        ]
    )
    got_a = [swap(sent_a[k], SEQ, 1 << orders[k][1]) for k in range(2)]
    d_normed_own, d_normed_got, mixed, held_bc, other_bc = after(
        (d_normed_own, d_normed_got, mixed, held_bc, other_bc), sent_a
    )
    full_c = assemble(held_bc[1], other_bc[1], SEQ, near[1][1], far + near[1][:1])
    d_normed = d_normed_own + d_normed_got
    own_unit = jnp.where(upper, unit_rows[:, share:], unit_rows[:, :share])
    own_gain = jnp.where(upper, prenorm_weight[share:], prenorm_weight[:share])
    own_rows = tokens.astype(f32)
    d_prenorm = jnp.sum(d_normed * own_unit, 0)
    d_unit_in = d_normed * own_gain
    mean_own = jnp.sum(d_unit_in * own_rows, -1)
    row_mean = ((mean_own + swap(mean_own, HEAD, 1)) / D)[:, None]
    input_gradient = (
        cotangent.astype(f32) + inverse * d_unit_in - own_rows * inverse**3 * row_mean
    )

    held_a = jnp.concatenate([k + g.astype(f32) for k, g in zip(kept_a, got_a)], 1)
    kept_a, sent_a = sides_of(held_a, SEQ, rest[0], rest)
    got_a = swap(sent_a, SEQ, 1 << rest[0])
    small, d_prenorm = after((small, d_prenorm[None]), sent_a)
    small = butterfly_sum(small, SEQ, orders[0][:2])
    d_prenorm = butterfly_sum(d_prenorm, SEQ, orders[0][:2])
    projected = own_features(back_product(mixed, full_c))
    output = (tokens.astype(f32) + projected).astype(bf16)
    held_a = kept_a + got_a.astype(f32)
    kept_a, sent_a = sides_of(held_a, SEQ, rest[1], rest[1:])
    got_a = swap(sent_a, SEQ, 1 << rest[1])
    prenorm_own = butterfly_sum(after(d_prenorm, sent_a), SEQ, rest)
    got_bc = after(got_bc, sent_a)
    if len(rest) > 1:
        held_bc_grad = [k + g.astype(f32) for k, g in zip(kept_bc, got_bc)]
    outer_grad, gate_grad = [scatter_rows(h, SEQ, rest[2:], rest[2:]) for h in held_bc_grad]
    outer_grad = outer_grad.T
    got_a = after(got_a, output, input_gradient)
    rest_grad = scatter_rows(kept_a + got_a.astype(f32), SEQ, rest[2:], rest[2:])
    filters_grad = small[: KC + 1, :value_width]
    probes_grad = small[: KC + 1, value_width:]
    postnorm_grad = small[KC + 1, :value_width]
    prenorm_grad = side_by_side(prenorm_own, swap(prenorm_own, HEAD, 1), upper)[0]
    heads_grad = small[KC + 2, : 3 * heads_local].reshape(3, heads_local)

    groups_grad = rest_grad[:, value_width:conv_width]
    stepper_grad = rest_grad[:, conv_width : conv_width + heads_local]
    root = math.sqrt(local_rows * seq_count)
    inner_new = update_inner(
        inner_weight, inner_velocity, inner_average, gate_grad, rest_grad, D ** (-0.5) / root
    )
    groups_new = apply_update(
        groups_weight, groups_velocity, groups_average, groups_grad, D ** (-0.5) / root
    )
    stepper_new = apply_update(
        stepper_weight, stepper_velocity, stepper_average, stepper_grad, (4 * D) ** (-0.5) / root
    )
    outer_new = apply_update(
        outer_weight, outer_velocity, outer_average, outer_grad, DI ** (-0.5) / root
    )
    filters_new = apply_update(
        filters_weight, filters_velocity, filters_average, filters_grad, 0.5 / root
    )
    probes_new = apply_update(
        probes_weight, probes_velocity, probes_average, probes_grad, 0.5 / root
    )
    prenorm_new = apply_update(
        prenorm_weight, prenorm_velocity, prenorm_average, prenorm_grad, 0.1 / root
    )
    postnorm_new = apply_update(
        postnorm_weight, postnorm_velocity, postnorm_average, postnorm_grad, 0.1 / root
    )
    heads_new = apply_update(heads_weight, heads_velocity, heads_average, heads_grad, 0.5 / root)
    return (
        output,
        input_gradient,
        inner_new[0],
        inner_new[1],
        inner_new[2],
        inner_new[3],
        groups_new[0],
        groups_new[1],
        groups_new[2],
        groups_new[3],
        stepper_new[0],
        stepper_new[1],
        stepper_new[2],
        stepper_new[3],
        outer_new[0],
        outer_new[1],
        outer_new[2],
        outer_new[3],
        filters_new[0],
        filters_new[1],
        filters_new[2],
        filters_new[3],
        probes_new[0],
        probes_new[1],
        probes_new[2],
        probes_new[3],
        prenorm_new[0],
        prenorm_new[1],
        prenorm_new[2],
        prenorm_new[3],
        postnorm_new[0],
        postnorm_new[1],
        postnorm_new[2],
        postnorm_new[3],
        heads_new[0],
        heads_new[1],
        heads_new[2],
        heads_new[3],
    )


def solution(mesh):
    return jax.shard_map(
        shards,
        mesh=mesh,
        in_specs=(
            P(SEQ, HEAD),
            P(SEQ, HEAD),
            P(SEQ),
            P(SEQ),
            P(SEQ, None, HEAD),
            P(SEQ, None, HEAD),
            P(SEQ, None, HEAD),
            P(SEQ, HEAD),
            P(SEQ, HEAD),
            P(SEQ, HEAD),
            P(SEQ, HEAD),
            P(SEQ, HEAD),
            P(SEQ, HEAD),
            P(HEAD, SEQ),
            P(HEAD, SEQ),
            P(HEAD, SEQ),
            P(None, HEAD),
            P(None, HEAD),
            P(None, HEAD),
            P(None, HEAD),
            P(None, HEAD),
            P(None, HEAD),
            P(),
            P(),
            P(),
            P(HEAD),
            P(HEAD),
            P(HEAD),
            P(None, HEAD),
            P(None, HEAD),
            P(None, HEAD),
        ),
        out_specs=(
            P(SEQ, HEAD),
            P(SEQ, HEAD),
            P(SEQ, None, HEAD),
            P(SEQ, None, HEAD),
            P(SEQ, None, HEAD),
            P(SEQ, None, HEAD),
            P(SEQ, HEAD),
            P(SEQ, HEAD),
            P(SEQ, HEAD),
            P(SEQ, HEAD),
            P(SEQ, HEAD),
            P(SEQ, HEAD),
            P(SEQ, HEAD),
            P(SEQ, HEAD),
            P(HEAD, SEQ),
            P(HEAD, SEQ),
            P(HEAD, SEQ),
            P(HEAD, SEQ),
            P(None, HEAD),
            P(None, HEAD),
            P(None, HEAD),
            P(None, HEAD),
            P(None, HEAD),
            P(None, HEAD),
            P(None, HEAD),
            P(None, HEAD),
            P(),
            P(),
            P(),
            P(),
            P(HEAD),
            P(HEAD),
            P(HEAD),
            P(HEAD),
            P(None, HEAD),
            P(None, HEAD),
            P(None, HEAD),
            P(None, HEAD),
        ),
        check_vma=False,
    )
```
